32 devices in a mesh: dp: 8 (over z, y), mp: 4 (over x, core).
Axes of the slice: x: 2, y: 2, z: 4, core: 2. Of those that a mesh axis runs over, the one named last changes fastest.
Arguments:
- grad_flat: bfloat16 [8, 5202320], P('dp', 'mp'), may hold values from -4 to 4
- error_flat: bfloat16 [8, 5202320], P('dp', 'mp'), may hold values from -2 to 2
- momentum_flat: float32 [5202320], P('mp'), may hold values from -2 to 2
- warm_x: float32 [3072, 32], replicated, may hold values from -6 to 6
- warm_b: float32 [128, 32], replicated, may hold values from -6 to 6
- warm_c: float32 [128, 32], replicated, may hold values from -6 to 6
- warm_dt: float32 [48, 32], replicated, may hold values from -6 to 6
- part_order: int32 [6], replicated, may hold values from 0 to 5, each once
Outputs:
- error_next: bfloat16 [8, 5202320], P('dp', 'mp')
- momentum_next: float32 [5202320], P('mp')
The draws below stay inside these ranges and needn't reach their ends.
Inputs may be any that keep to these rules, and one draw needn't show every extreme that they name: `part_order`: each part number appears once.
All inputs are finite; a program needn't handle non-finite values.
Results may differ from the reference program's by a relative error of at most 0.0017.
Values sent between devices are 32-bit elements; how exact they have to be, the bound alone decides.
No kernel may reach another device: no remote copies, remote signals or barrier semaphores. Data moves between devices by JAX's collectives and lax.ppermute only.
A program may use at most 64 MiB of HBM per device.

```python
import jax
import jax.numpy as jnp
from jax import lax

D = 1536
DI = 3072
DS = 128
NH = 48
KW = 4
RANK = 32
NS_STEPS = 5
CONV_CH = 3328
VEC = 3472
FLAT_DEV = 1300580
FLAT = 5202320
N_DP = 8
N_MP = 4


def draw_grad_flat(key, part):
    shared = jax.random.normal(jax.random.fold_in(key, 11), (1, FLAT), jnp.float32)
    single = jax.random.normal(jax.random.fold_in(key, 12), (N_DP, FLAT), jnp.float32)
    values = 0.8 * shared + 0.6 * single
    return jnp.clip(values, -4.0, 4.0).astype(jnp.bfloat16)


def block_scale(stream_key, extent, pieces, smallest, largest):
    def one(dim, blocks):
        draws = jax.random.uniform(jax.random.fold_in(jax.random.fold_in(stream_key, 6), dim), (blocks,), jnp.float32, smallest / len(pieces), largest / len(pieces))
        return jnp.repeat(jnp.exp(draws), extent[dim] // blocks).reshape((-1,) + (1,) * (len(extent) - dim - 1))

    level = one(*pieces[0])
    for cut in pieces[1:]:
        level = level * one(*cut)
    return level


def centred(stream_key, dims, scale, reach, pieces=(), kind=jnp.bfloat16):
    result = jax.random.normal(stream_key, dims, jnp.float32) * scale
    if len(pieces) > 0:
        result = block_scale(stream_key, dims, pieces, -0.22, 0.18) * result
    return jnp.clip(result, min=-reach, max=reach).astype(kind)


def setup_inputs(seed: int = 0) -> dict:
    splits = jax.random.split(jax.random.key(seed), 9)
    return {
        "grad_flat": draw_grad_flat(jax.random.fold_in(splits[8], 71), 0),
        "error_flat": centred(splits[1], (N_DP, FLAT), 0.3, 2.0, ((0, 8), (1, 4))),
        "momentum_flat": centred(splits[2], (FLAT,), 0.3, 2.0, ((0, 4),), jnp.float32),
        "warm_x": centred(splits[3], (DI, RANK), 1.0, 6.0, (), jnp.float32),
        "warm_b": centred(splits[4], (DS, RANK), 1.0, 6.0, (), jnp.float32),
        "warm_c": centred(splits[5], (DS, RANK), 1.0, 6.0, (), jnp.float32),
        "warm_dt": centred(splits[6], (NH, RANK), 1.0, 6.0, (), jnp.float32),
        "part_order": jax.random.permutation(splits[7], 6).astype(jnp.int32),
    }


precise = lax.Precision.HIGHEST
momentum_decay = 0.9
ns_first = 3.4445
ns_second = -4.775
ns_third = 2.0315

def shard_sizes(blocks):
    return [D * DI // blocks, D * DS // blocks, D * DS // blocks, D * NH // blocks, CONV_CH * KW // blocks, VEC // blocks]

def shard_offsets(part_order, sizes):
    table = jnp.array(sizes, dtype=jnp.int32)
    labels = jnp.arange(6, dtype=jnp.int32)
    placed = lax.optimization_barrier(jnp.sum(jnp.where(part_order[None, :] == labels[:, None], labels[None, :], 0), axis=1)).astype(jnp.int32)
    earlier = placed[None, :] < placed[:, None]
    return lax.optimization_barrier(jnp.sum(jnp.where(earlier, table[None, :], 0), axis=1)).astype(jnp.int32)

def orthonormal(panel):
    frame = panel / (jnp.sqrt(jnp.sum(panel * panel)) + 1e-06)
    for _ in range(NS_STEPS):
        gram = jnp.dot(frame.T, frame, precision=precise)
        mixing = ns_first * jnp.eye(gram.shape[0], dtype=jnp.float32) + ns_second * gram + ns_third * jnp.dot(gram, gram, precision=precise)
        frame = jnp.dot(frame, mixing, precision=precise)
    return frame

def reference(grad_flat, error_flat, momentum_flat, warm_x, warm_b, warm_c, warm_dt, part_order):
    sizes = shard_sizes(N_MP)
    starts = shard_offsets(part_order, sizes)
    merged = (grad_flat.astype(jnp.float32) + error_flat.astype(jnp.float32)).reshape(N_DP, N_MP, FLAT_DEV)
    moment = momentum_flat.reshape(N_MP, FLAT_DEV)
    error_out = jnp.zeros((N_DP, N_MP, FLAT_DEV), jnp.bfloat16)
    moment_out = jnp.zeros((N_MP, FLAT_DEV), jnp.float32)
    widths = [DI, DS, DS, NH]
    warms = [warm_x, warm_b, warm_c, warm_dt]
    for member in range(4):
        piece = lax.dynamic_slice_in_dim(merged, starts[member], sizes[member], 2)
        matrix = piece.reshape(N_DP, D, widths[member])
        panel = jnp.einsum('nrc,cq->rq', matrix, warms[member], precision=precise)
        frame = orthonormal(panel)
        factor = jnp.einsum('nrc,rq->cq', matrix, frame, precision=precise)
        approx = jnp.dot(frame, factor.T, precision=precise) / N_DP
        residue = (matrix - approx[None]).astype(jnp.bfloat16).reshape(N_DP, N_MP, sizes[member])
        error_out = lax.dynamic_update_slice_in_dim(error_out, residue, starts[member], 2)
        previous = lax.dynamic_slice_in_dim(moment, starts[member], sizes[member], 1)
        updated = momentum_decay * previous + approx.reshape(N_MP, sizes[member])
        moment_out = lax.dynamic_update_slice_in_dim(moment_out, updated, starts[member], 1)
    for member in (4, 5):
        piece = lax.dynamic_slice_in_dim(merged, starts[member], sizes[member], 2)
        average = lax.optimization_barrier(jnp.sum(piece, axis=0)) / N_DP
        previous = lax.dynamic_slice_in_dim(moment, starts[member], sizes[member], 1)
        moment_out = lax.dynamic_update_slice_in_dim(moment_out, momentum_decay * previous + average, starts[member], 1)
    return (error_out.reshape(N_DP, FLAT), moment_out.reshape(FLAT))
```

```python
import functools

import jax
import jax.numpy as jnp
from jax import lax
from jax.experimental import pallas as pl
from jax.experimental.pallas import tpu as pltpu
from jax.sharding import PartitionSpec as P

D = 1536
DI = 3072
DS = 128
NH = 48
KW = 4
RANK = 32
NS_STEPS = 5
CONV_CH = 3328
VEC = 3472
LANES = 128

momentum_decay = 0.9
ns_first = 3.4445
ns_second = -4.775
ns_third = 2.0315

COL_B = DI
COL_C = DI + DS
COL_DT = DI + 2 * DS
COLS = DI + 3 * DS
GRAM = COLS
WIDE = COLS + LANES
CHUNKS = DI // LANES

f32 = jnp.float32
bf16 = jnp.bfloat16


class Plan:
    def __init__(self, blocks):
        self.rows = D // blocks
        self.sizes = [
            D * DI // blocks,
            D * DS // blocks,
            D * DS // blocks,
            D * NH // blocks,
            CONV_CH * KW // blocks,
            VEC // blocks,
        ]
        self.total = sum(self.sizes)
        self.flat_rows = -(-self.total // LANES)
        self.buf_rows = (self.flat_rows + 15) // 8 * 8 + 16
        self.dt_groups = self.rows // 8
        self.conv_rows = self.sizes[4] // LANES
        self.conv_pad = -(-self.conv_rows // 8) * 8
        self.vec_rows = -(-self.sizes[5] // LANES)
        self.vec_pad = -(-self.vec_rows // 8) * 8
        self.panel_rows = self.rows + self.conv_pad + self.vec_pad


def starts_of(order_ref, sizes):
    zero = jnp.int32(0)
    first = [zero] * 6
    run = zero
    for place in range(6):
        part = order_ref[place]
        size = zero
        for k in range(6):
            here = part == k
            first[k] = jnp.where(here, run, first[k])
            size = jnp.where(here, jnp.int32(sizes[k]), size)
        run = run + size
    return [lax.shift_right_logical(o, 7) for o in first], [jnp.bitwise_and(o, 127) for o in first]


def lane_of(shape):
    return lax.broadcasted_iota(jnp.int32, shape, len(shape) - 1)


def split2(x):
    hi = x.astype(bf16)
    return hi, (x - hi.astype(f32)).astype(bf16)


def split3(x):
    hi = x.astype(bf16)
    rest = x - hi.astype(f32)
    mid = rest.astype(bf16)
    return hi, mid, (rest - mid.astype(f32)).astype(bf16)


def dot_nt(a, b):
    return lax.dot_general(a, b, (((1,), (1,)), ((), ())), preferred_element_type=f32)


def dot_tn(a, b):
    return lax.dot_general(a, b, (((0,), (0,)), ((), ())), preferred_element_type=f32)


def dot_exact(a, b):
    return lax.dot_general(
        a, b, (((1,), (0,)), ((), ())), preferred_element_type=f32, precision=lax.Precision.HIGHEST
    )


def spread(x, group):
    x = jnp.where(lane_of(x.shape) // RANK == group, x, 0.0)
    x = x + pltpu.roll(x, 64, 1)
    return x + pltpu.roll(x, 32, 1)


def panel_kernel(plan, order_ref, g_ref, e_ref, wx_ref, wb_ref, wc_ref, wd_ref, pp_ref, mh_ref, ml_ref, m_ref, dt_ref, w_ref):
    rows = plan.rows
    total = plan.total

    def merged(at, width):
        return g_ref[0:1, pl.ds(at, width)].astype(f32) + e_ref[0:1, pl.ds(at, width)].astype(f32)

    full = total // 1024
    unroll = 8

    def merge(i, _):
        for u in range(unroll):
            at = pl.multiple_of(i * (1024 * unroll), 1024) + 1024 * u
            m_ref[pl.ds(pl.multiple_of(i * (8 * unroll), 8) + 8 * u, 8), :] = merged(at, 1024).reshape(8, LANES)
        return 0

    lax.fori_loop(0, full // unroll, merge, 0)
    for i in range(full // unroll * unroll, full):
        m_ref[8 * i : 8 * i + 8, :] = merged(1024 * i, 1024).reshape(8, LANES)
    for r in range(8 * full, total // LANES):
        m_ref[r : r + 1, :] = merged(LANES * r, LANES)
    rest = total % LANES
    if rest:
        r = total // LANES
        m_ref[r : r + 1, 0:rest] = merged(LANES * r, rest)

    row, lane = starts_of(order_ref, plan.sizes)

    def turn(x, s):
        return pltpu.roll(x, jnp.bitwise_and(LANES - s, 127), 1)

    def put(at, column, tile):
        hi, lo = split2(tile)
        mh_ref[pl.ds(at, 16), column : column + LANES] = hi
        ml_ref[pl.ds(at, 16), column : column + LANES] = lo

    keep16 = lane_of((16, LANES))

    def read_x(i, _):
        base = row[0] + i * (16 * CHUNKS)
        keep = keep16 < LANES - lane[0]
        now = turn(m_ref[pl.ds(base, 16, stride=CHUNKS), :], lane[0])
        for c in range(CHUNKS):
            after = turn(m_ref[pl.ds(base + (c + 1), 16, stride=CHUNKS), :], lane[0])
            put(pl.multiple_of(i * 16, 16), c * LANES, jnp.where(keep, now, after))
            now = after
        return 0

    lax.fori_loop(0, rows // 16, read_x, 0)

    def read_bc(i, _):
        for k, column in ((1, COL_B), (2, COL_C)):
            base = row[k] + i * 16
            now = turn(m_ref[pl.ds(base, 16), :], lane[k])
            after = turn(m_ref[pl.ds(base + 1, 16), :], lane[k])
            put(pl.multiple_of(i * 16, 16), column, jnp.where(keep16 < LANES - lane[k], now, after))
        return 0

    lax.fori_loop(0, rows // 16, read_bc, 0)

    groups = plan.dt_groups
    lanes_dt = lane_of((groups, LANES))
    thirds = [turn(m_ref[pl.ds(row[3] + q, groups, stride=3), :], lane[3]) for q in range(4)]
    thirds = [jnp.where(lanes_dt < LANES - lane[3], thirds[q], thirds[q + 1]) for q in range(3)]
    for b in range(8):
        q, s = divmod(NH * b, LANES)
        piece = thirds[q] if s == 0 else pltpu.roll(thirds[q], LANES - s, 1)
        if s + NH > LANES:
            piece = jnp.where(lanes_dt < LANES - s, piece, pltpu.roll(thirds[q + 1], LANES - s, 1))
        dt_ref[b * groups : (b + 1) * groups, :] = jnp.where(lanes_dt < NH, piece, 0.0)

    def read_dt(i, _):
        at = pl.multiple_of(i * 16, 16)
        put(at, COL_DT, dt_ref[pl.ds(at, 16), :])
        return 0

    lax.fori_loop(0, rows // 16, read_dt, 0)

    shape = (plan.conv_pad, LANES)
    now = turn(m_ref[pl.ds(row[4], plan.conv_pad), :], lane[4])
    after = turn(m_ref[pl.ds(row[4] + 1, plan.conv_pad), :], lane[4])
    conv = jnp.where(lane_of(shape) < LANES - lane[4], now, after)
    conv = jnp.where(lax.broadcasted_iota(jnp.int32, shape, 0) < plan.conv_rows, conv, 0.0)
    pp_ref[rows : rows + plan.conv_pad, :] = conv
    shape = (plan.vec_pad, LANES)
    place = lax.broadcasted_iota(jnp.int32, shape, 0) * LANES + lane_of(shape)
    vec = jnp.where(place < plan.sizes[5], m_ref[pl.ds(row[5], plan.vec_pad), :], 0.0)
    pp_ref[rows + plan.conv_pad :, :] = vec

    w_ref[...] = jnp.zeros_like(w_ref)
    w_ref[:, 0:NH] = wd_ref[...]
    panel = None
    lanes = lane_of((rows, LANES))
    for k, (w, column, width) in enumerate(
        ((wx_ref, 0, DI), (wb_ref, COL_B, DS), (wc_ref, COL_C, DS), (w_ref, COL_DT, LANES))
    ):
        hi, mid, lo = split3(w[...])
        none = jnp.zeros_like(hi)
        part = dot_nt(mh_ref[:, column : column + width], jnp.concatenate([hi, mid, lo, none], 0))
        part = part + dot_nt(ml_ref[:, column : column + width], jnp.concatenate([hi, mid, none, none], 0))
        part = part + pltpu.roll(part, 64, 1)
        part = part + pltpu.roll(part, 32, 1)
        panel = part if k == 0 else jnp.where(lanes >= RANK * k, part, panel)
    pp_ref[0:rows, :] = panel


def factor_kernel(plan, replicas, pp_ref, mh_ref, ml_ref, z_ref):
    rows = plan.rows
    panel = pp_ref[0:rows, :]
    group = lane_of((rows, LANES)) // RANK
    for k, column, width in ((0, 0, DI), (1, COL_B, DS), (2, COL_C, DS), (3, COL_DT, DS)):
        hi, mid, lo = (piece.astype(f32) for piece in split3(spread(panel, k)))
        two = jnp.where(group == 0, hi, jnp.where(group == 1, mid, 0.0))
        three = jnp.where(group == 2, lo, two).astype(bf16)
        two = two.astype(bf16)
        step = min(width, 512)

        def block(at):
            z = dot_tn(three, mh_ref[:, pl.ds(at, step)]) + dot_tn(two, ml_ref[:, pl.ds(at, step)])
            z_ref[:, pl.ds(at, step)] = z[0:32] + z[32:64] + z[64:96]

        if width == step:
            block(column)
        else:
            lax.fori_loop(0, width // step, lambda i, _: (block(pl.multiple_of(i * step, step)), 0)[1], 0)
    gram = lax.dot_general(
        panel, panel, (((0,), (0,)), ((), ())), preferred_element_type=f32, precision=lax.Precision.HIGHEST
    )
    group = lane_of((RANK, LANES)) // RANK
    out = gram[0:RANK]
    for k in range(1, 4):
        out = jnp.where(group == k, gram[RANK * k : RANK * (k + 1)], out)
    z_ref[:, GRAM : GRAM + LANES] = out * (1.0 / replicas)


def output_kernel(plan, replicas, order_ref, z_ref, pp_ref, m_ref, mom_ref, err_ref, next_ref, a_ref, x_ref, s_ref):
    rows = plan.rows
    row, lane = starts_of(order_ref, plan.sizes)

    square = (LANES, LANES)
    down = lax.broadcasted_iota(jnp.int32, square, 0)
    along = lane_of(square)
    same = down // RANK == along // RANK
    eye = jnp.where(down == along, 1.0, 0.0)
    ones = jnp.where(same, 1.0, 0.0)
    gram = z_ref[:, GRAM : GRAM + LANES]
    gram = jnp.where(same, jnp.concatenate([gram] * 4, 0), 0.0)
    trace = dot_exact(dot_exact(ones, gram * eye), ones)
    scale = 1.0 / (jnp.sqrt(trace) + 1e-06)
    scale = jnp.where(same, scale * scale, 0.0)
    gram = gram * scale
    turned = eye
    for step in range(NS_STEPS):
        mixing = ns_first * eye + ns_second * gram + ns_third * dot_exact(gram, gram)
        turned = dot_exact(turned, mixing)
        if step + 1 < NS_STEPS:
            gram = dot_exact(mixing, dot_exact(gram, mixing))
    both = lax.dot_general(
        turned, turned, (((1,), (1,)), ((), ())), preferred_element_type=f32, precision=lax.Precision.HIGHEST
    )
    left = dot_exact(pp_ref[0:rows, :], both * (scale * (1.0 / replicas)))

    group = lane_of((rows, LANES)) // RANK
    for k, column, width in ((0, 0, DI), (1, COL_B, DS), (2, COL_C, DS), (3, COL_DT, DS)):
        hi, mid = (piece.astype(f32) for piece in split2(spread(left, k)))
        lhs = jnp.where(group % 2 == 0, hi, mid).astype(bf16)
        step = min(width, 512)

        def block(at):
            hi, mid = split2(z_ref[:, pl.ds(at, step)])
            rhs = jnp.concatenate([hi, hi, mid, mid], 0)
            x_ref[:, pl.ds(at, step)] = lax.dot_general(
                lhs, rhs, (((1,), (0,)), ((), ())), preferred_element_type=f32
            )

        if width == step:
            block(column)
        else:
            lax.fori_loop(0, width // step, lambda i, _: (block(pl.multiple_of(i * step, step)), 0)[1], 0)

    lanes8 = lane_of((8, LANES))
    first8 = lax.broadcasted_iota(jnp.int32, (8, LANES), 0) == 0
    lanes1 = lane_of((1, LANES))

    def write_x(i, last):
        at = pl.multiple_of(i * 8, 8)
        base = row[0] + i * (8 * CHUNKS)
        keep = lanes8 >= lane[0]
        head = turned0 = pltpu.roll(x_ref[pl.ds(at, 8), 0:LANES], lane[0], 1)
        for c in range(1, CHUNKS):
            now = pltpu.roll(x_ref[pl.ds(at, 8), c * LANES : (c + 1) * LANES], lane[0], 1)
            a_ref[pl.ds(base + c, 8, stride=CHUNKS), :] = jnp.where(keep, now, head)
            head = now
        tail = pltpu.roll(head, 1, 0)
        a_ref[pl.ds(base, 8, stride=CHUNKS), :] = jnp.where(keep, turned0, jnp.where(first8, last, tail))
        return tail

    lax.fori_loop(0, rows // 8, write_x, jnp.zeros((8, LANES), f32))
    last_x = pltpu.roll(x_ref[rows - 8 : rows, DI - LANES : DI], lane[0], 1)[7:8]
    end_x = row[0] + rows * CHUNKS
    a_ref[pl.ds(end_x, 1), :] = jnp.where(lanes1 < lane[0], last_x, a_ref[pl.ds(end_x, 1), :])

    def place(k, count, valid):
        s = lane[k]
        head = pltpu.roll(s_ref[8:16, :], s, 1)[0:1]
        end = pltpu.roll(s_ref[count : count + 8, :], s, 1)[7:8]
        if valid == LANES:
            a_ref[pl.ds(row[k], 1), :] = jnp.where(lanes1 >= s, head, a_ref[pl.ds(row[k], 1), :])
            final = row[k] + count
            a_ref[pl.ds(final, 1), :] = jnp.where(lanes1 < s, end, a_ref[pl.ds(final, 1), :])
            for r in range(1, count, 64):
                n = min(64, count - r)
                now = pltpu.roll(s_ref[8 + r : 8 + r + n, :], s, 1)
                before = pltpu.roll(s_ref[7 + r : 7 + r + n, :], s, 1)
                a_ref[pl.ds(row[k] + r, n), :] = jnp.where(lane_of((n, LANES)) >= s, now, before)
        else:
            a_ref[pl.ds(row[k], count - 1), :] = s_ref[8 : 8 + count - 1, :]
            final = row[k] + count - 1
            end = s_ref[8 + count - 1 : 8 + count, :]
            a_ref[pl.ds(final, 1), :] = jnp.where(lanes1 < valid, end, a_ref[pl.ds(final, 1), :])

    s_ref[8 : 8 + rows, :] = x_ref[:, COL_B : COL_B + DS]
    place(1, rows, LANES)
    s_ref[8 : 8 + rows, :] = x_ref[:, COL_C : COL_C + DS]
    place(2, rows, LANES)
    groups = plan.dt_groups
    lanes_dt = lane_of((groups, LANES))
    for q in range(3):
        third = jnp.zeros((groups, LANES), f32)
        for b in range(8):
            lo = NH * b - LANES * q
            if lo <= -NH or lo >= LANES:
                continue
            piece = x_ref[b * groups : (b + 1) * groups, COL_DT : COL_DT + LANES]
            if lo % LANES:
                piece = pltpu.roll(piece, lo % LANES, 1)
            third = jnp.where((lanes_dt >= lo) & (lanes_dt < lo + NH), piece, third)
        s_ref[pl.ds(8 + q, groups, stride=3), :] = third
    place(3, 3 * groups, LANES)
    s_ref[8 : 8 + plan.conv_pad, :] = pp_ref[rows : rows + plan.conv_pad, :] * (1.0 / replicas)
    place(4, plan.conv_rows, LANES)
    s_ref[8 : 8 + plan.vec_pad, :] = pp_ref[rows + plan.conv_pad :, :] * (1.0 / replicas)
    place(5, plan.vec_rows, plan.sizes[5] - (plan.vec_rows - 1) * LANES)

    total = plan.total
    begin4 = row[4] * LANES + lane[4]
    begin5 = row[5] * LANES + lane[5]

    def finish(at_row, count, width):
        n = count * LANES if count > 1 else width
        at = at_row * LANES
        m = m_ref[pl.ds(at_row, count), 0 : n // count]
        a = a_ref[pl.ds(at_row, count), 0 : n // count]
        index = lax.broadcasted_iota(jnp.int32, m.shape, 0) * LANES + lane_of(m.shape) + at
        in4 = (index >= begin4) & (index < begin4 + plan.sizes[4])
        in5 = (index >= begin5) & (index < begin5 + plan.sizes[5])
        err = jnp.where(in4 | in5, 0.0, m - a)
        err_ref[0:1, pl.ds(at, n)] = err.reshape(1, n).astype(bf16)
        next_ref[pl.ds(at, n)] = momentum_decay * mom_ref[pl.ds(at, n)] + a.reshape(n)

    full = total // 1024
    unroll = 4

    def step(i, _):
        for u in range(unroll):
            finish(pl.multiple_of(i * (8 * unroll), 8) + 8 * u, 8, LANES)
        return 0

    lax.fori_loop(0, full // unroll, step, 0)
    for i in range(full // unroll * unroll, full):
        finish(8 * i, 8, LANES)
    for r in range(8 * full, total // LANES):
        finish(r, 1, LANES)
    if total % LANES:
        finish(total // LANES, 1, total % LANES)


def vmem(count):
    return [pl.BlockSpec(memory_space=pltpu.VMEM)] * count


def call(kernel, order, out_shape, ins, scratch, limit, flops, size):
    specs = ([pl.BlockSpec(memory_space=pltpu.SMEM)] if order is not None else []) + vmem(len(ins))
    args = ([order] if order is not None else []) + list(ins)
    return pl.pallas_call(
        kernel,
        out_shape=out_shape,
        in_specs=specs,
        out_specs=tuple(vmem(len(out_shape))),
        scratch_shapes=scratch,
        compiler_params=pltpu.CompilerParams(vmem_limit_bytes=limit),
        cost_estimate=pl.CostEstimate(flops=flops, bytes_accessed=size, transcendentals=0),
    )(*args)


def exchange(x, axis, bit):
    n = lax.axis_size(axis)
    return lax.ppermute(x, axis, [(i, i ^ bit) for i in range(n)])


def bits(n):
    return [1 << b for b in range((n - 1).bit_length())]


def body(grad_flat, error_flat, momentum_flat, warm_x, warm_b, warm_c, warm_dt, part_order):
    plan = Plan(lax.axis_size("mp"))
    replicas = lax.axis_size("dp")
    rows = plan.rows
    shape = jax.ShapeDtypeStruct
    pp, mh, ml, m = call(
        functools.partial(panel_kernel, plan),
        part_order,
        (
            shape((plan.panel_rows, LANES), f32),
            shape((rows, COLS), bf16),
            shape((rows, COLS), bf16),
            shape((plan.buf_rows, LANES), f32),
        ),
        (grad_flat, error_flat, warm_x.T, warm_b.T, warm_c.T, warm_dt.T),
        [pltpu.VMEM((rows, LANES), f32), pltpu.VMEM((RANK, LANES), f32)],
        40 << 20,
        4 * rows * COLS * LANES,
        6 * plan.total * 4,
    )
    for bit in bits(replicas):
        pp = pp + exchange(pp, "dp", bit)
    (z,) = call(
        functools.partial(factor_kernel, plan, replicas),
        None,
        (shape((RANK, WIDE), f32),),
        (pp, mh, ml),
        [],
        32 << 20,
        4 * rows * COLS * LANES,
        plan.total * 4,
    )
    for bit in bits(lax.axis_size("mp")):
        z = z + exchange(z, "mp", bit)
    for bit in bits(replicas):
        z = z + exchange(z, "dp", bit)
    err, following = call(
        functools.partial(output_kernel, plan, replicas),
        part_order,
        (shape((1, plan.total), bf16), shape((plan.total,), f32)),
        (z, pp, m, momentum_flat),
        [
            pltpu.VMEM((plan.buf_rows, LANES), f32),
            pltpu.VMEM((rows, COLS), f32),
            pltpu.VMEM((rows + 24, LANES), f32),
        ],
        40 << 20,
        2 * rows * COLS * LANES,
        4 * plan.total * 4,
    )
    return err, following


def solution(mesh):
    placed = (P("dp", "mp"), P("dp", "mp"), P("mp"), P(), P(), P(), P(), P())
    return jax.shard_map(
        body, mesh=mesh, in_specs=placed, out_specs=(P("dp", "mp"), P("mp")), check_vma=False
    )
```

```python
import functools

import jax
import jax.numpy as jnp
from jax import lax
from jax.experimental import pallas as pl
from jax.experimental.pallas import tpu as pltpu
from jax.sharding import PartitionSpec as P

D = 1536
DI = 3072
DS = 128
NH = 48
KW = 4
RANK = 32
NS_STEPS = 5
CONV_CH = 3328
VEC = 3472
LANES = 128

momentum_decay = 0.9
ns_first = 3.4445
ns_second = -4.775
ns_third = 2.0315

COL_B = DI
COL_C = DI + DS
COL_DT = DI + 2 * DS
COLS = DI + 3 * DS
GRAM = COLS
WIDE = COLS + LANES
CHUNKS = DI // LANES

MERGE = 256
FINISH = 128
PIECES = 8

f32 = jnp.float32
bf16 = jnp.bfloat16
HBM = pltpu.MemorySpace.HBM
VMEM = pltpu.MemorySpace.VMEM


class Plan:
    def __init__(self, blocks):
        self.rows = D // blocks
        self.sizes = [
            D * DI // blocks,
            D * DS // blocks,
            D * DS // blocks,
            D * NH // blocks,
            CONV_CH * KW // blocks,
            VEC // blocks,
        ]
        self.total = sum(self.sizes)
        self.flat_rows = -(-self.total // LANES)
        self.buf_rows = (self.flat_rows + 15) // 8 * 8 + 16
        self.dt_groups = self.rows // 8
        self.conv_rows = self.sizes[4] // LANES
        self.conv_pad = -(-self.conv_rows // 8) * 8
        self.vec_rows = -(-self.sizes[5] // LANES)
        self.vec_pad = -(-self.vec_rows // 8) * 8
        self.panel_rows = self.rows + self.conv_pad + self.vec_pad
        self.shift = self.sizes[5] % LANES
        self.half = -(-self.panel_rows // 16) * 8
        step = -(-self.flat_rows // (PIECES * MERGE)) * MERGE
        cuts = list(range(0, self.flat_rows, step)) + [self.flat_rows]
        self.pieces = list(zip(cuts, cuts[1:]))


def starts_of(order_ref, sizes):
    zero = jnp.int32(0)
    first = [zero] * 6
    run = zero
    for place in range(6):
        part = order_ref[place]
        size = zero
        for k in range(6):
            here = part == k
            first[k] = jnp.where(here, run, first[k])
            size = jnp.where(here, jnp.int32(sizes[k]), size)
        run = run + size
    return [lax.shift_right_logical(o, 7) for o in first], [jnp.bitwise_and(o, 127) for o in first]


def lane_of(shape):
    return lax.broadcasted_iota(jnp.int32, shape, len(shape) - 1)


def split2(x):
    hi = x.astype(bf16)
    return hi, (x - hi.astype(f32)).astype(bf16)


def split3(x):
    hi = x.astype(bf16)
    rest = x - hi.astype(f32)
    mid = rest.astype(bf16)
    return hi, mid, (rest - mid.astype(f32)).astype(bf16)


def dot_nt(a, b):
    return lax.dot_general(a, b, (((1,), (1,)), ((), ())), preferred_element_type=f32)


def dot_tn(a, b):
    return lax.dot_general(a, b, (((0,), (0,)), ((), ())), preferred_element_type=f32)


def dot_exact(a, b):
    return lax.dot_general(
        a, b, (((1,), (0,)), ((), ())), preferred_element_type=f32, precision=lax.Precision.HIGHEST
    )


def spread(x, group):
    x = jnp.where(lane_of(x.shape) // RANK == group, x, 0.0)
    x = x + pltpu.roll(x, 64, 1)
    return x + pltpu.roll(x, 32, 1)


def panel_kernel(plan, order_hbm, g_hbm, e_hbm, wx_hbm, wb_hbm, wc_hbm, wd_hbm, top_ref, low_ref, mh_ref, ml_ref, m_ref, order_ref, g_ref, e_ref, wx_ref, wb_ref, wc_ref, wd_ref, dt_ref, w_ref, sems):
    rows = plan.rows
    total = plan.total
    shift = plan.shift

    small = [
        pltpu.make_async_copy(src, dst, sems.at[i])
        for i, (src, dst) in enumerate(
            ((order_hbm, order_ref), (wx_hbm, wx_ref), (wb_hbm, wb_ref), (wc_hbm, wc_ref), (wd_hbm, wd_ref))
        )
    ]
    big = []
    for i, (begin, end) in enumerate(plan.pieces):
        part = (slice(0, 1), slice(begin * LANES, min(end * LANES, total)))
        big.append(
            [
                pltpu.make_async_copy(src.at[part], dst.at[part], sems.at[5 + 2 * i + j])
                for j, (src, dst) in enumerate(((g_hbm, g_ref), (e_hbm, e_ref)))
            ]
        )
    for i, pair in enumerate(big):
        for copy in pair:
            copy.start()
        if i == 0:
            for copy in small:
                copy.start()

    def merged(at, width):
        return g_ref[0:1, pl.ds(at, width)].astype(f32) + e_ref[0:1, pl.ds(at, width)].astype(f32)

    for (begin, end), pair in zip(plan.pieces, big):
        for copy in pair:
            copy.wait()
        whole = min(end, total // LANES)

        def merge(i, _):
            r = pl.multiple_of(begin + i * MERGE, 8)
            m_ref[pl.ds(r, MERGE), :] = merged(pl.multiple_of(r * LANES, 1024), MERGE * LANES).reshape(MERGE, LANES)
            return 0

        count = (whole - begin) // MERGE
        lax.fori_loop(0, count, merge, 0)
        r = begin + count * MERGE
        n = (whole - r) // 8 * 8
        if n:
            m_ref[r : r + n, :] = merged(r * LANES, n * LANES).reshape(n, LANES)
        for r in range(r + n, whole):
            m_ref[r : r + 1, :] = merged(LANES * r, LANES)
        if end > whole:
            m_ref[whole : whole + 1, 0 : total % LANES] = merged(LANES * whole, total % LANES)

    for copy in small:
        copy.wait()
    row, lane = starts_of(order_ref, plan.sizes)

    def fetch(base, count, stride, moved):
        step = {} if stride == 1 else {"stride": stride}
        now = m_ref[pl.ds(base, count, **step), :]
        return pltpu.roll(now, LANES - shift, 1) if moved else now

    def joined(base, count, stride, moved):
        now = fetch(base, count, stride, moved)
        if not moved:
            return now
        return jnp.where(lane_of((count, LANES)) < LANES - shift, now, fetch(base + 1, count, stride, moved))

    def either(k, work):
        for moved in (False, True):
            pl.when((lane[k] != 0) == moved)(functools.partial(work, moved))

    def put(at, count, column, tile):
        hi, lo = split2(tile)
        mh_ref[pl.ds(at, count), column : column + LANES] = hi
        ml_ref[pl.ds(at, count), column : column + LANES] = lo

    high = 32

    def read_x(moved):
        keep = lane_of((high, LANES)) < LANES - shift

        def block(i, _):
            base = row[0] + i * (high * CHUNKS)
            at = pl.multiple_of(i * high, high)
            now = fetch(base, high, CHUNKS, moved)
            for c in range(CHUNKS):
                tile = now
                if moved or c + 1 < CHUNKS:
                    now = fetch(base + (c + 1), high, CHUNKS, moved)
                if moved:
                    tile = jnp.where(keep, tile, now)
                put(at, high, c * LANES, tile)
            return 0

        lax.fori_loop(0, rows // high, block, 0)

    either(0, read_x)
    for k, column in ((1, COL_B), (2, COL_C)):
        either(k, lambda moved, k=k, column=column: put(0, rows, column, joined(row[k], rows, 1, moved)))

    groups = plan.dt_groups
    lanes_dt = lane_of((groups, LANES))

    def read_dt(moved):
        thirds = [joined(row[3] + q, groups, 3, moved) for q in range(3)]
        for b in range(8):
            q, s = divmod(NH * b, LANES)
            piece = thirds[q] if s == 0 else pltpu.roll(thirds[q], LANES - s, 1)
            if s + NH > LANES:
                piece = jnp.where(lanes_dt < LANES - s, piece, pltpu.roll(thirds[q + 1], LANES - s, 1))
            dt_ref[b * groups : (b + 1) * groups, :] = jnp.where(lanes_dt < NH, piece, 0.0)

    either(3, read_dt)
    put(0, rows, COL_DT, dt_ref[...])

    low = rows - plan.half

    def read_conv(moved):
        shape = (plan.conv_pad, LANES)
        conv = joined(row[4], plan.conv_pad, 1, moved)
        conv = jnp.where(lax.broadcasted_iota(jnp.int32, shape, 0) < plan.conv_rows, conv, 0.0)
        low_ref[low : low + plan.conv_pad, :] = conv

    either(4, read_conv)
    shape = (plan.vec_pad, LANES)
    place = lax.broadcasted_iota(jnp.int32, shape, 0) * LANES + lane_of(shape)
    vec = jnp.where(place < plan.sizes[5], m_ref[pl.ds(row[5], plan.vec_pad), :], 0.0)
    low_ref[low + plan.conv_pad :, :] = vec

    w_ref[...] = jnp.zeros_like(w_ref)
    w_ref[:, 0:NH] = wd_ref[...]
    panel = None
    lanes = lane_of((rows, LANES))
    for k, (w, column, width) in enumerate(
        ((wx_ref, 0, DI), (wb_ref, COL_B, DS), (wc_ref, COL_C, DS), (w_ref, COL_DT, LANES))
    ):
        hi, mid, lo = split3(w[...])
        none = jnp.zeros_like(hi)
        part = dot_nt(mh_ref[:, column : column + width], jnp.concatenate([hi, mid, lo, none], 0))
        part = part + dot_nt(ml_ref[:, column : column + width], jnp.concatenate([hi, mid, none, none], 0))
        part = part + pltpu.roll(part, 64, 1)
        part = part + pltpu.roll(part, 32, 1)
        panel = part if k == 0 else jnp.where(lanes >= RANK * k, part, panel)
    top_ref[...] = panel[0 : plan.half]
    low_ref[0:low, :] = panel[plan.half :]


def factor_kernel(plan, replicas, top_ref, low_ref, mh_ref, ml_ref, mine0_ref, mine1_ref, other_ref, z_ref):
    rows = plan.rows
    panel = jnp.concatenate([top_ref[...], low_ref[0 : rows - plan.half, :]], 0)
    group = lane_of((rows, LANES)) // RANK
    for k, column, width in ((0, 0, DI), (1, COL_B, DS), (2, COL_C, DS), (3, COL_DT, DS)):
        hi, mid, lo = (piece.astype(f32) for piece in split3(spread(panel, k)))
        two = jnp.where(group == 0, hi, jnp.where(group == 1, mid, 0.0))
        three = jnp.where(group == 2, lo, two).astype(bf16)
        two = two.astype(bf16)
        z = dot_tn(three, mh_ref[:, column : column + width]) + dot_tn(two, ml_ref[:, column : column + width])
        z_ref[:, column : column + width] = z[0:32] + z[32:64] + z[64:96]
    gram = lax.dot_general(
        panel, panel, (((0,), (0,)), ((), ())), preferred_element_type=f32, precision=lax.Precision.HIGHEST
    )
    group = lane_of((RANK, LANES)) // RANK
    out = gram[0:RANK]
    for k in range(1, 4):
        out = jnp.where(group == k, gram[RANK * k : RANK * (k + 1)], out)
    z_ref[:, GRAM : GRAM + LANES] = out * (1.0 / replicas)
    half = RANK // 2
    core = jnp.bitwise_and(lax.axis_index("mp"), 1)
    for mine in (0, 1):

        @pl.when(core == mine)
        def _():
            mine0_ref[...] = z_ref[half * mine : half * mine + half // 2, :]
            mine1_ref[...] = z_ref[half * mine + half // 2 : half * (mine + 1), :]
            other_ref[...] = z_ref[half * (1 - mine) : half * (2 - mine), :]


def output_kernel(plan, replicas, order_ref, mine0_ref, mine1_ref, other0_ref, other1_ref, top_ref, low_ref, m_ref, mom_ref, err_hbm, next_hbm, z_ref, a_ref, x_ref, s_ref, err_ref, next_ref, sems):
    rows = plan.rows
    shift = plan.shift
    row, lane = starts_of(order_ref, plan.sizes)

    quarter = RANK // 4
    core = jnp.bitwise_and(lax.axis_index("mp"), 1)
    for mine in (0, 1):

        @pl.when(core == mine)
        def _():
            for i, ref in enumerate((mine0_ref, mine1_ref, other0_ref, other1_ref)):
                at = (2 * mine + i) % 4 * quarter
                z_ref[at : at + quarter, :] = ref[...]

    square = (LANES, LANES)
    down = lax.broadcasted_iota(jnp.int32, square, 0)
    along = lane_of(square)
    same = down // RANK == along // RANK
    eye = jnp.where(down == along, 1.0, 0.0)
    ones = jnp.where(same, 1.0, 0.0)
    gram = z_ref[:, GRAM : GRAM + LANES]
    gram = jnp.where(same, jnp.concatenate([gram] * 4, 0), 0.0)
    trace = dot_exact(dot_exact(ones, gram * eye), ones)
    scale = 1.0 / (jnp.sqrt(trace) + 1e-06)
    scale = jnp.where(same, scale * scale, 0.0)
    gram = gram * scale
    turned = eye
    for step in range(NS_STEPS):
        mixing = ns_first * eye + ns_second * gram + ns_third * dot_exact(gram, gram)
        turned = dot_exact(turned, mixing)
        if step + 1 < NS_STEPS:
            gram = dot_exact(mixing, dot_exact(gram, mixing))
    both = lax.dot_general(
        turned, turned, (((1,), (1,)), ((), ())), preferred_element_type=f32, precision=lax.Precision.HIGHEST
    )
    panel = jnp.concatenate([top_ref[...], low_ref[0 : rows - plan.half, :]], 0)
    left = dot_exact(panel, both * (scale * (1.0 / replicas)))

    group = lane_of((rows, LANES)) // RANK
    for k, column, width in ((0, 0, DI), (1, COL_B, DS), (2, COL_C, DS), (3, COL_DT, DS)):
        hi, mid = (piece.astype(f32) for piece in split2(spread(left, k)))
        lhs = jnp.where(group % 2 == 0, hi, mid).astype(bf16)
        hi, mid = split2(z_ref[:, column : column + width])
        rhs = jnp.concatenate([hi, hi, mid, mid], 0)
        x_ref[8 : 8 + rows, column : column + width] = lax.dot_general(
            lhs, rhs, (((1,), (0,)), ((), ())), preferred_element_type=f32
        )

    high = 32
    lanes1 = lane_of((1, LANES))

    def right(x):
        return pltpu.roll(x, shift, 1)

    def either(k, work):
        for moved in (False, True):
            pl.when((lane[k] != 0) == moved)(functools.partial(work, moved))

    def write_x(moved):
        keep = lane_of((high, LANES)) >= shift
        if moved:
            s_ref[8 : 8 + rows, :] = right(x_ref[8 : 8 + rows, DI - LANES : DI])

        def block(i, _):
            at = pl.multiple_of(8 + i * high, 8)
            base = row[0] + i * (high * CHUNKS)
            if moved:
                before = s_ref[pl.ds(at - 1, high), :]
            for c in range(CHUNKS):
                now = x_ref[pl.ds(at, high), c * LANES : (c + 1) * LANES]
                if moved:
                    now = right(now)
                    now, before = jnp.where(keep, now, before), now
                a_ref[pl.ds(base + c, high, stride=CHUNKS), :] = now
            return 0

        lax.fori_loop(0, rows // high, block, 0)
        if moved:
            final = row[0] + rows * CHUNKS
            end = s_ref[rows + 7 : rows + 8, :]
            a_ref[pl.ds(final, 1), :] = jnp.where(lanes1 < shift, end, a_ref[pl.ds(final, 1), :])

    either(0, write_x)

    def place(k, ref, column, count):
        columns = slice(column, column + LANES)

        def work(moved):
            if not moved:
                a_ref[pl.ds(row[k], count), :] = ref[8 : 8 + count, columns]
                return
            head = right(ref[8:16, columns])[0:1]
            end = right(ref[count : count + 8, columns])[7:8]
            a_ref[pl.ds(row[k], 1), :] = jnp.where(lanes1 >= shift, head, a_ref[pl.ds(row[k], 1), :])
            final = row[k] + count
            a_ref[pl.ds(final, 1), :] = jnp.where(lanes1 < shift, end, a_ref[pl.ds(final, 1), :])
            n = count - 1
            now = right(ref[9 : 9 + n, columns])
            before = right(ref[8 : 8 + n, columns])
            a_ref[pl.ds(row[k] + 1, n), :] = jnp.where(lane_of((n, LANES)) >= shift, now, before)

        either(k, work)

    place(1, x_ref, COL_B, rows)
    place(2, x_ref, COL_C, rows)
    groups = plan.dt_groups
    lanes_dt = lane_of((groups, LANES))
    for q in range(3):
        third = jnp.zeros((groups, LANES), f32)
        for b in range(8):
            lo = NH * b - LANES * q
            if lo <= -NH or lo >= LANES:
                continue
            piece = x_ref[8 + b * groups : 8 + (b + 1) * groups, COL_DT : COL_DT + LANES]
            if lo % LANES:
                piece = pltpu.roll(piece, lo % LANES, 1)
            third = jnp.where((lanes_dt >= lo) & (lanes_dt < lo + NH), piece, third)
        s_ref[pl.ds(8 + q, groups, stride=3), :] = third
    place(3, s_ref, 0, 3 * groups)
    low = rows - plan.half
    s_ref[8 : 8 + plan.conv_pad, :] = low_ref[low : low + plan.conv_pad, :] * (1.0 / replicas)
    place(4, s_ref, 0, plan.conv_rows)
    vec = low_ref[low + plan.conv_pad :, :] * (1.0 / replicas)
    last = plan.vec_rows - 1
    a_ref[pl.ds(row[5], last), :] = vec[0:last]
    final = row[5] + last
    valid = plan.sizes[5] - last * LANES
    a_ref[pl.ds(final, 1), :] = jnp.where(lanes1 < valid, vec[last : last + 1], a_ref[pl.ds(final, 1), :])

    total = plan.total
    spans = [(row[k] * LANES + lane[k], row[k] * LANES + lane[k] + plan.sizes[k]) for k in (4, 5)]

    def finish(at_row, count, width=LANES):
        n = count * width
        at = at_row * LANES
        a = a_ref[pl.ds(at_row, count), 0:width]
        next_ref[pl.ds(at, n)] = momentum_decay * mom_ref[pl.ds(at, n)] + a.reshape(n)
        near = [(at < end) & (at + n > begin) for begin, end in spans]
        near = near[0] | near[1]

        @pl.when(jnp.logical_not(near))
        def _():
            err = m_ref[pl.ds(at_row, count), 0:width] - a_ref[pl.ds(at_row, count), 0:width]
            err_ref[0:1, pl.ds(at, n)] = err.astype(bf16).reshape(1, n)

        @pl.when(near)
        def _():
            err = m_ref[pl.ds(at_row, count), 0:width] - a_ref[pl.ds(at_row, count), 0:width]
            index = lax.broadcasted_iota(jnp.int32, err.shape, 0) * LANES + lane_of(err.shape) + at
            for begin, end in spans:
                err = jnp.where((index >= begin) & (index < end), 0.0, err)
            err_ref[0:1, pl.ds(at, n)] = err.astype(bf16).reshape(1, n)

    copies = []
    for i, (begin, end) in enumerate(plan.pieces):
        whole = min(end, total // LANES)
        count = (whole - begin) // FINISH
        lax.fori_loop(0, count, lambda j, _: (finish(pl.multiple_of(begin + j * FINISH, 8), FINISH), 0)[1], 0)
        r = begin + count * FINISH
        n = (whole - r) // 8 * 8
        if n:
            finish(r, n)
        for r in range(r + n, whole):
            finish(r, 1)
        if end > whole:
            finish(whole, 1, total % LANES)
        part = slice(begin * LANES, min(end * LANES, total))
        copies.append(pltpu.make_async_copy(err_ref.at[0:1, part], err_hbm.at[0:1, part], sems.at[2 * i]))
        copies.append(pltpu.make_async_copy(next_ref.at[part], next_hbm.at[part], sems.at[2 * i + 1]))
        for copy in copies[-2:]:
            copy.start()
    for copy in copies:
        copy.wait()


def specs(*spaces):
    return [pl.BlockSpec(memory_space=space) for space in spaces]


def pairwise(x, first, second):
    n = lax.axis_size("dp") * lax.axis_size("mp")
    return lax.ppermute(x, ("dp", "mp"), [(i, i ^ (second if i % 2 else first)) for i in range(n)])


def butterfly(halves, steps, turns):
    n = len(steps)
    order = [[steps[(i + t) % n] for i in range(n)] for t in turns]
    for i in range(n):
        got = [pairwise(halves[h], order[2 * h][i], order[2 * h + 1][i]) for h in (0, 1)]
        halves = [mine + other for mine, other in zip(halves, got)]
    return halves


def body(grad_flat, error_flat, momentum_flat, warm_x, warm_b, warm_c, warm_dt, part_order):
    blocks = lax.axis_size("mp")
    replicas = lax.axis_size("dp")
    plan = Plan(blocks)
    rows = plan.rows
    total = plan.total
    shape = jax.ShapeDtypeStruct
    pieces = len(plan.pieces)
    dma = pltpu.SemaphoreType.DMA
    top, low, mh, ml, m = pl.pallas_call(
        functools.partial(panel_kernel, plan),
        out_shape=(
            shape((plan.half, LANES), f32),
            shape((plan.panel_rows - plan.half, LANES), f32),
            shape((rows, COLS), bf16),
            shape((rows, COLS), bf16),
            shape((plan.buf_rows, LANES), f32),
        ),
        in_specs=specs(*[HBM] * 7),
        out_specs=tuple(specs(*[VMEM] * 5)),
        scratch_shapes=[
            pltpu.SMEM((6,), jnp.int32),
            pltpu.VMEM((1, total), bf16),
            pltpu.VMEM((1, total), bf16),
            pltpu.VMEM((RANK, DI), f32),
            pltpu.VMEM((RANK, DS), f32),
            pltpu.VMEM((RANK, DS), f32),
            pltpu.VMEM((RANK, NH), f32),
            pltpu.VMEM((rows, LANES), f32),
            pltpu.VMEM((RANK, LANES), f32),
            dma((5 + 2 * pieces,)),
        ],
        compiler_params=pltpu.CompilerParams(vmem_limit_bytes=36 << 20),
        cost_estimate=pl.CostEstimate(flops=4 * rows * COLS * LANES, bytes_accessed=8 * total, transcendentals=0),
    )(*(pltpu.with_memory_space_constraint(x, HBM) for x in (part_order, grad_flat, error_flat, warm_x.T, warm_b.T, warm_c.T, warm_dt.T)))

    inner = [1 << b for b in range(1, (blocks - 1).bit_length())]
    outer = [blocks << b for b in range((replicas - 1).bit_length())]
    n = len(outer)
    top, low = butterfly([top, low], outer, (0, n - 1, 1, 0))

    mine0, mine1, other = pl.pallas_call(
        functools.partial(factor_kernel, plan, replicas),
        out_shape=(shape((RANK // 4, WIDE), f32), shape((RANK // 4, WIDE), f32), shape((RANK // 2, WIDE), f32)),
        in_specs=specs(*[VMEM] * 4),
        out_specs=tuple(specs(*[VMEM] * 3)),
        scratch_shapes=[pltpu.VMEM((RANK, WIDE), f32)],
        compiler_params=pltpu.CompilerParams(vmem_limit_bytes=24 << 20),
        cost_estimate=pl.CostEstimate(flops=4 * rows * COLS * LANES, bytes_accessed=4 * total, transcendentals=0),
    )(top, low, mh, ml)
    got = pairwise(other, 1, 1)
    steps = inner + outer
    n = len(steps)
    halves = butterfly(
        [mine0 + got[: RANK // 4], mine1 + got[RANK // 4 :]], steps, (0, n // 2, 1, 1 + n // 2)
    )
    others = [pairwise(half, 1, 1) for half in halves]

    return pl.pallas_call(
        functools.partial(output_kernel, plan, replicas),
        out_shape=(shape((1, total), bf16), shape((total,), f32)),
        in_specs=specs(pltpu.SMEM, *[VMEM] * 8),
        out_specs=tuple(specs(HBM, HBM)),
        scratch_shapes=[
            pltpu.VMEM((RANK, WIDE), f32),
            pltpu.VMEM((plan.buf_rows, LANES), f32),
            pltpu.VMEM((rows + 8, COLS), f32),
            pltpu.VMEM((rows + 24, LANES), f32),
            pltpu.VMEM((1, total), bf16),
            pltpu.VMEM((total,), f32),
            dma((2 * pieces,)),
        ],
        compiler_params=pltpu.CompilerParams(vmem_limit_bytes=36 << 20),
        cost_estimate=pl.CostEstimate(flops=2 * rows * COLS * LANES, bytes_accessed=16 * total, transcendentals=0),
    )(part_order, *halves, *others, top, low, m, momentum_flat)


def solution(mesh):
    placed = (P("dp", "mp"), P("dp", "mp"), P("mp"), P(), P(), P(), P(), P())
    return jax.shard_map(
        body, mesh=mesh, in_specs=placed, out_specs=(P("dp", "mp"), P("mp")), check_vma=False
    )
```

```python
import functools

import jax
import jax.numpy as jnp
from jax import lax
from jax.experimental import pallas as pl
from jax.experimental.pallas import tpu as pltpu
from jax.sharding import PartitionSpec as P

D = 1536
DI = 3072
DS = 128
NH = 48
KW = 4
RANK = 32
NS_STEPS = 5
CONV_CH = 3328
VEC = 3472
LANES = 128

momentum_decay = 0.9
ns_first = 3.4445
ns_second = -4.775
ns_third = 2.0315

COL_B = DI
COL_C = DI + DS
COL_DT = DI + 2 * DS
COLS = DI + 3 * DS
WITH_GRAM = COLS + 4 * LANES
CHUNKS = DI // LANES

MERGE = 256
FINISH = 128
PIECES = 8

f32 = jnp.float32
bf16 = jnp.bfloat16
HBM = pltpu.MemorySpace.HBM
VMEM = pltpu.MemorySpace.VMEM


class Plan:
    def __init__(self, blocks):
        self.rows = D // blocks
        self.sizes = [
            D * DI // blocks,
            D * DS // blocks,
            D * DS // blocks,
            D * NH // blocks,
            CONV_CH * KW // blocks,
            VEC // blocks,
        ]
        self.total = sum(self.sizes)
        self.flat_rows = -(-self.total // LANES)
        self.buf_rows = (self.flat_rows + 15) // 8 * 8 + 16
        self.dt_groups = self.rows // 8
        self.conv_rows = self.sizes[4] // LANES
        self.conv_pad = -(-self.conv_rows // 8) * 8
        self.vec_rows = -(-self.sizes[5] // LANES)
        self.vec_pad = -(-self.vec_rows // 8) * 8
        self.panel_rows = self.rows + self.conv_pad + self.vec_pad
        self.shift = self.sizes[5] % LANES
        self.half = -(-self.panel_rows // 16) * 8
        step = -(-self.flat_rows // (PIECES * MERGE)) * MERGE
        cuts = list(range(0, self.flat_rows, step)) + [self.flat_rows]
        self.pieces = list(zip(cuts, cuts[1:]))


def starts_of(order_ref, sizes):
    zero = jnp.int32(0)
    first = [zero] * 6
    run = zero
    for place in range(6):
        part = order_ref[place]
        size = zero
        for k in range(6):
            here = part == k
            first[k] = jnp.where(here, run, first[k])
            size = jnp.where(here, jnp.int32(sizes[k]), size)
        run = run + size
    return [lax.shift_right_logical(o, 7) for o in first], [jnp.bitwise_and(o, 127) for o in first]


def lane_of(shape):
    return lax.broadcasted_iota(jnp.int32, shape, len(shape) - 1)


def split2(x):
    hi = x.astype(bf16)
    return hi, (x - hi.astype(f32)).astype(bf16)


def split3(x):
    hi = x.astype(bf16)
    rest = x - hi.astype(f32)
    mid = rest.astype(bf16)
    return hi, mid, (rest - mid.astype(f32)).astype(bf16)


def dot_nt(a, b):
    return lax.dot_general(a, b, (((1,), (1,)), ((), ())), preferred_element_type=f32)


def dot_tn(a, b):
    return lax.dot_general(a, b, (((0,), (0,)), ((), ())), preferred_element_type=f32)


def dot_exact(a, b):
    return lax.dot_general(
        a, b, (((1,), (0,)), ((), ())), preferred_element_type=f32, precision=lax.Precision.HIGHEST
    )


def spread(x, group):
    x = jnp.where(lane_of(x.shape) // RANK == group, x, 0.0)
    x = x + pltpu.roll(x, 64, 1)
    return x + pltpu.roll(x, 32, 1)


def panel_kernel(plan, order_hbm, g_hbm, e_hbm, wx_hbm, wb_hbm, wc_hbm, wd_hbm, top_ref, low_ref, mh_ref, ml_ref, m_ref, order_ref, g_ref, e_ref, wx_ref, wb_ref, wc_ref, wd_ref, dt_ref, w_ref, sems):
    rows = plan.rows
    total = plan.total
    shift = plan.shift

    small = [
        pltpu.make_async_copy(src, dst, sems.at[i])
        for i, (src, dst) in enumerate(
            ((order_hbm, order_ref), (wx_hbm, wx_ref), (wb_hbm, wb_ref), (wc_hbm, wc_ref), (wd_hbm, wd_ref))
        )
    ]
    big = []
    for i, (begin, end) in enumerate(plan.pieces):
        part = (slice(0, 1), slice(begin * LANES, min(end * LANES, total)))
        big.append(
            [
                pltpu.make_async_copy(src.at[part], dst.at[part], sems.at[5 + 2 * i + j])
                for j, (src, dst) in enumerate(((g_hbm, g_ref), (e_hbm, e_ref)))
            ]
        )
    small[0].start()
    for i, pair in enumerate(big):
        for copy in pair:
            copy.start()
        if i == 0:
            for copy in small[1:]:
                copy.start()
    small[0].wait()
    row, lane = starts_of(order_ref, plan.sizes)

    def merged(at, width):
        return g_ref[0:1, pl.ds(at, width)].astype(f32) + e_ref[0:1, pl.ds(at, width)].astype(f32)

    def fetch(base, count, stride, moved):
        step = {} if stride == 1 else {"stride": stride}
        now = m_ref[pl.ds(base, count, **step), :]
        return pltpu.roll(now, LANES - shift, 1) if moved else now

    def joined(base, count, stride, moved):
        now = fetch(base, count, stride, moved)
        if not moved:
            return now
        return jnp.where(lane_of((count, LANES)) < LANES - shift, now, fetch(base + 1, count, stride, moved))

    def either(k, work):
        for moved in (False, True):
            pl.when((lane[k] != 0) == moved)(functools.partial(work, moved))

    def put(at, count, column, tile):
        hi, lo = split2(tile)
        mh_ref[pl.ds(at, count), column : column + LANES] = hi
        ml_ref[pl.ds(at, count), column : column + LANES] = lo

    high = 32

    def read_x(first, last, moved):
        keep = lane_of((high, LANES)) < LANES - shift

        def block(i, _):
            base = row[0] + i * (high * CHUNKS)
            at = pl.multiple_of(i * high, high)
            now = fetch(base, high, CHUNKS, moved)
            for c in range(CHUNKS):
                tile = now
                if moved or c + 1 < CHUNKS:
                    now = fetch(base + (c + 1), high, CHUNKS, moved)
                if moved:
                    tile = jnp.where(keep, tile, now)
                put(at, high, c * LANES, tile)
            return 0

        lax.fori_loop(first, last, block, 0)

    done = 0
    for (begin, end), pair in zip(plan.pieces, big):
        for copy in pair:
            copy.wait()
        whole = min(end, total // LANES)

        def merge(i, _):
            r = pl.multiple_of(begin + i * MERGE, 8)
            m_ref[pl.ds(r, MERGE), :] = merged(pl.multiple_of(r * LANES, 1024), MERGE * LANES).reshape(MERGE, LANES)
            return 0

        count = (whole - begin) // MERGE
        lax.fori_loop(0, count, merge, 0)
        r = begin + count * MERGE
        n = (whole - r) // 8 * 8
        if n:
            m_ref[r : r + n, :] = merged(r * LANES, n * LANES).reshape(n, LANES)
        for r in range(r + n, whole):
            m_ref[r : r + 1, :] = merged(LANES * r, LANES)
        if end > whole:
            m_ref[whole : whole + 1, 0 : total % LANES] = merged(LANES * whole, total % LANES)

        ready = rows // high
        if end < plan.flat_rows:
            ready = jnp.minimum(lax.div(jnp.maximum(end - 1 - row[0], 0), jnp.int32(high * CHUNKS)), rows // high)
        either(0, functools.partial(read_x, done, ready))
        done = ready
    for copy in small[1:]:
        copy.wait()
    for k, column in ((1, COL_B), (2, COL_C)):
        either(k, lambda moved, k=k, column=column: put(0, rows, column, joined(row[k], rows, 1, moved)))

    groups = plan.dt_groups
    lanes_dt = lane_of((groups, LANES))

    def read_dt(moved):
        thirds = [joined(row[3] + q, groups, 3, moved) for q in range(3)]
        for b in range(8):
            q, s = divmod(NH * b, LANES)
            piece = thirds[q] if s == 0 else pltpu.roll(thirds[q], LANES - s, 1)
            if s + NH > LANES:
                piece = jnp.where(lanes_dt < LANES - s, piece, pltpu.roll(thirds[q + 1], LANES - s, 1))
            dt_ref[b * groups : (b + 1) * groups, :] = jnp.where(lanes_dt < NH, piece, 0.0)

    either(3, read_dt)
    put(0, rows, COL_DT, dt_ref[...])

    low = rows - plan.half

    def read_conv(moved):
        shape = (plan.conv_pad, LANES)
        conv = joined(row[4], plan.conv_pad, 1, moved)
        conv = jnp.where(lax.broadcasted_iota(jnp.int32, shape, 0) < plan.conv_rows, conv, 0.0)
        low_ref[low : low + plan.conv_pad, :] = conv

    either(4, read_conv)
    shape = (plan.vec_pad, LANES)
    place = lax.broadcasted_iota(jnp.int32, shape, 0) * LANES + lane_of(shape)
    vec = jnp.where(place < plan.sizes[5], m_ref[pl.ds(row[5], plan.vec_pad), :], 0.0)
    low_ref[low + plan.conv_pad :, :] = vec

    w_ref[...] = jnp.zeros_like(w_ref)
    w_ref[:, 0:NH] = wd_ref[...]
    panel = None
    lanes = lane_of((rows, LANES))
    for k, (w, column, width) in enumerate(
        ((wx_ref, 0, DI), (wb_ref, COL_B, DS), (wc_ref, COL_C, DS), (w_ref, COL_DT, LANES))
    ):
        hi, mid, lo = split3(w[...])
        none = jnp.zeros_like(hi)
        part = dot_nt(mh_ref[:, column : column + width], jnp.concatenate([hi, mid, lo, none], 0))
        part = part + dot_nt(ml_ref[:, column : column + width], jnp.concatenate([hi, mid, none, none], 0))
        part = part + pltpu.roll(part, 64, 1)
        part = part + pltpu.roll(part, 32, 1)
        panel = part if k == 0 else jnp.where(lanes >= RANK * k, part, panel)
    top_ref[...] = panel[0 : plan.half]
    low_ref[0:low, :] = panel[plan.half :]


def factor_kernel(plan, top_ref, low_ref, mh_ref, ml_ref, mine0_ref, mine1_ref, other_ref, z_ref):
    rows = plan.rows
    panel = jnp.concatenate([top_ref[...], low_ref[0 : rows - plan.half, :]], 0)
    group = lane_of((rows, LANES)) // RANK
    for k, column, width in ((0, 0, DI), (1, COL_B, DS), (2, COL_C, DS), (3, COL_DT, DS)):
        hi, mid, lo = (piece.astype(f32) for piece in split3(spread(panel, k)))
        two = jnp.where(group == 0, hi, jnp.where(group == 1, mid, 0.0))
        three = jnp.where(group == 2, lo, two).astype(bf16)
        two = two.astype(bf16)
        z = dot_tn(three, mh_ref[:, column : column + width]) + dot_tn(two, ml_ref[:, column : column + width])
        z_ref[:, column : column + width] = z[0:32] + z[32:64] + z[64:96]
    gram = lax.dot_general(
        panel, panel, (((0,), (0,)), ((), ())), preferred_element_type=f32, precision=lax.Precision.HIGHEST
    )
    group = lane_of((RANK, LANES)) // RANK
    out = gram[0:RANK]
    for k in range(1, 4):
        out = jnp.where(group == k, gram[RANK * k : RANK * (k + 1)], out)
    half = RANK // 2
    core = jnp.bitwise_and(lax.axis_index("mp"), 1)
    for mine in (0, 1):

        @pl.when(core == mine)
        def _():
            mine0_ref[:, 0:COLS] = z_ref[half * mine : half * mine + half // 2, :]
            mine1_ref[...] = z_ref[half * mine + half // 2 : half * (mine + 1), :]
            other_ref[:, 0:COLS] = z_ref[half * (1 - mine) : half * (2 - mine), :]

    other_ref[:, COLS:] = jnp.zeros((half, 4 * LANES), f32)
    for b in range(4):
        lanes = slice(COLS + b * LANES, COLS + (b + 1) * LANES)
        mine0_ref[:, lanes] = out[8 * b : 8 * (b + 1)]
        other_ref[0:8, lanes] = out[8 * b : 8 * (b + 1)]


def block_masks():
    square = (LANES, LANES)
    down = lax.broadcasted_iota(jnp.int32, square, 0)
    along = lane_of(square)
    return jnp.where(down == along, 1.0, 0.0), jnp.where(down // RANK == along // RANK, 1.0, 0.0)


def newton_schulz(eye, gram, turned, steps, last):
    for step in range(steps):
        mixing = ns_first * eye + ns_second * gram + ns_third * dot_exact(gram, gram)
        turned = mixing if turned is None else dot_exact(turned, mixing)
        if not (last and step + 1 == steps):
            gram = dot_exact(mixing, dot_exact(gram, mixing))
    return gram, turned


def begin_kernel(sum_ref, gram_out, turned_out, scale_out):
    eye, ones = block_masks()
    gram = [sum_ref[:, b * LANES : (b + 1) * LANES] for b in range(4)]
    gram = jnp.concatenate(gram * 4, 0) * ones
    trace = jnp.sum(gram * eye, axis=0, keepdims=True)
    trace = dot_exact(jnp.broadcast_to(trace, (8, LANES)), ones)
    scale = 1.0 / (jnp.sqrt(trace) + 1e-06)
    scale = scale * scale
    scale_out[...] = scale
    gram_out[...], turned_out[...] = newton_schulz(eye, gram * scale[0:1], None, NS_STEPS // 2, False)


def frame_kernel(plan, replicas, gram_ref, turned_ref, scale_ref, top_ref, low_ref, lhs_ref):
    rows = plan.rows
    eye, _ = block_masks()
    _, turned = newton_schulz(eye, gram_ref[...], turned_ref[...], NS_STEPS - NS_STEPS // 2, True)
    both = lax.dot_general(
        turned, turned, (((1,), (1,)), ((), ())), preferred_element_type=f32, precision=lax.Precision.HIGHEST
    )
    panel = jnp.concatenate([top_ref[...], low_ref[0 : rows - plan.half, :]], 0)
    left = dot_exact(panel, both * (scale_ref[0:1] * (1.0 / replicas)))
    group = lane_of((rows, LANES)) // RANK
    for k in range(4):
        hi, mid = (piece.astype(f32) for piece in split2(spread(left, k)))
        lhs_ref[k * rows : (k + 1) * rows, :] = jnp.where(group % 2 == 0, hi, mid).astype(bf16)


def output_kernel(plan, replicas, order_ref, mine0_ref, mine1_ref, other0_ref, other1_ref, lhs_ref, low_ref, m_ref, mom_ref, err_hbm, next_hbm, z_ref, a_ref, x_ref, s_ref, err_ref, next_ref, sems):
    rows = plan.rows
    shift = plan.shift
    row, lane = starts_of(order_ref, plan.sizes)

    quarter = RANK // 4
    core = jnp.bitwise_and(lax.axis_index("mp"), 1)
    for mine in (0, 1):

        @pl.when(core == mine)
        def _():
            for i, ref in enumerate((mine0_ref, mine1_ref, other0_ref, other1_ref)):
                at = (2 * mine + i) % 4 * quarter
                z_ref[at : at + quarter, :] = ref[...]

    for k, column, width in ((0, 0, DI), (1, COL_B, DS), (2, COL_C, DS), (3, COL_DT, DS)):
        lhs = lhs_ref[k * rows : (k + 1) * rows, :]
        hi, mid = split2(z_ref[:, column : column + width])
        rhs = jnp.concatenate([hi, hi, mid, mid], 0)
        x_ref[8 : 8 + rows, column : column + width] = lax.dot_general(
            lhs, rhs, (((1,), (0,)), ((), ())), preferred_element_type=f32
        )

    high = 32
    lanes1 = lane_of((1, LANES))

    def right(x):
        return pltpu.roll(x, shift, 1)

    def either(k, work):
        for moved in (False, True):
            pl.when((lane[k] != 0) == moved)(functools.partial(work, moved))

    def write_x(first, last, moved):
        keep = lane_of((high, LANES)) >= shift

        def block(i, _):
            at = pl.multiple_of(8 + i * high, 8)
            base = row[0] + i * (high * CHUNKS)
            if moved:
                before = s_ref[pl.ds(at - 1, high), :]
            for c in range(CHUNKS):
                now = x_ref[pl.ds(at, high), c * LANES : (c + 1) * LANES]
                if moved:
                    now = right(now)
                    now, before = jnp.where(keep, now, before), now
                a_ref[pl.ds(base + c, high, stride=CHUNKS), :] = now
            return 0

        lax.fori_loop(first, last, block, 0)


    def place(k, ref, column, count):
        columns = slice(column, column + LANES)

        def work(moved):
            if not moved:
                a_ref[pl.ds(row[k], count), :] = ref[8 : 8 + count, columns]
                return
            head = right(ref[8:16, columns])[0:1]
            end = right(ref[count : count + 8, columns])[7:8]
            a_ref[pl.ds(row[k], 1), :] = jnp.where(lanes1 >= shift, head, a_ref[pl.ds(row[k], 1), :])
            final = row[k] + count
            a_ref[pl.ds(final, 1), :] = jnp.where(lanes1 < shift, end, a_ref[pl.ds(final, 1), :])
            n = count - 1
            now = right(ref[9 : 9 + n, columns])
            before = right(ref[8 : 8 + n, columns])
            a_ref[pl.ds(row[k] + 1, n), :] = jnp.where(lane_of((n, LANES)) >= shift, now, before)

        either(k, work)

    place(1, x_ref, COL_B, rows)
    place(2, x_ref, COL_C, rows)
    groups = plan.dt_groups
    lanes_dt = lane_of((groups, LANES))
    for q in range(3):
        third = jnp.zeros((groups, LANES), f32)
        for b in range(8):
            lo = NH * b - LANES * q
            if lo <= -NH or lo >= LANES:
                continue
            piece = x_ref[8 + b * groups : 8 + (b + 1) * groups, COL_DT : COL_DT + LANES]
            if lo % LANES:
                piece = pltpu.roll(piece, lo % LANES, 1)
            third = jnp.where((lanes_dt >= lo) & (lanes_dt < lo + NH), piece, third)
        s_ref[pl.ds(8 + q, groups, stride=3), :] = third
    place(3, s_ref, 0, 3 * groups)
    low = rows - plan.half
    s_ref[8 : 8 + plan.conv_pad, :] = low_ref[low : low + plan.conv_pad, :] * (1.0 / replicas)
    place(4, s_ref, 0, plan.conv_rows)
    vec = low_ref[low + plan.conv_pad :, :] * (1.0 / replicas)
    last = plan.vec_rows - 1
    a_ref[pl.ds(row[5], last), :] = vec[0:last]
    final = row[5] + last
    valid = plan.sizes[5] - last * LANES
    a_ref[pl.ds(final, 1), :] = jnp.where(lanes1 < valid, vec[last : last + 1], a_ref[pl.ds(final, 1), :])

    @pl.when(lane[0] != 0)
    def _():
        s_ref[8 : 8 + rows, :] = right(x_ref[8 : 8 + rows, DI - LANES : DI])
        s_ref[7:8, :] = a_ref[pl.ds(row[0], 1), :]
        final = row[0] + rows * CHUNKS
        end = s_ref[rows + 7 : rows + 8, :]
        a_ref[pl.ds(final, 1), :] = jnp.where(lanes1 < shift, end, a_ref[pl.ds(final, 1), :])

    total = plan.total
    spans = [(row[k] * LANES + lane[k], row[k] * LANES + lane[k] + plan.sizes[k]) for k in (4, 5)]

    def finish(at_row, count, width=LANES):
        n = count * width
        at = at_row * LANES
        a = a_ref[pl.ds(at_row, count), 0:width]
        next_ref[pl.ds(at, n)] = momentum_decay * mom_ref[pl.ds(at, n)] + a.reshape(n)
        near = [(at < end) & (at + n > begin) for begin, end in spans]
        near = near[0] | near[1]

        @pl.when(jnp.logical_not(near))
        def _():
            err = m_ref[pl.ds(at_row, count), 0:width] - a_ref[pl.ds(at_row, count), 0:width]
            err_ref[0:1, pl.ds(at, n)] = err.astype(bf16).reshape(1, n)

        @pl.when(near)
        def _():
            err = m_ref[pl.ds(at_row, count), 0:width] - a_ref[pl.ds(at_row, count), 0:width]
            index = lax.broadcasted_iota(jnp.int32, err.shape, 0) * LANES + lane_of(err.shape) + at
            for begin, end in spans:
                err = jnp.where((index >= begin) & (index < end), 0.0, err)
            err_ref[0:1, pl.ds(at, n)] = err.astype(bf16).reshape(1, n)

    copies = []
    done = 0
    for i, (begin, end) in enumerate(plan.pieces):
        step = high * CHUNKS
        ready = rows // high
        if end < plan.flat_rows:
            ready = jnp.minimum(lax.div(jnp.maximum(end - row[0], 0) + (step - 1), jnp.int32(step)), rows // high)
        either(0, functools.partial(write_x, done, ready))
        done = ready
        whole = min(end, total // LANES)
        count = (whole - begin) // FINISH
        lax.fori_loop(0, count, lambda j, _: (finish(pl.multiple_of(begin + j * FINISH, 8), FINISH), 0)[1], 0)
        r = begin + count * FINISH
        n = (whole - r) // 8 * 8
        if n:
            finish(r, n)
        for r in range(r + n, whole):
            finish(r, 1)
        if end > whole:
            finish(whole, 1, total % LANES)
        part = slice(begin * LANES, min(end * LANES, total))
        copies.append(pltpu.make_async_copy(err_ref.at[0:1, part], err_hbm.at[0:1, part], sems.at[2 * i]))
        copies.append(pltpu.make_async_copy(next_ref.at[part], next_hbm.at[part], sems.at[2 * i + 1]))
        for copy in copies[-2:]:
            copy.start()
    for copy in copies:
        copy.wait()


def specs(*spaces):
    return [pl.BlockSpec(memory_space=space) for space in spaces]


def pairwise(x, first, second):
    n = lax.axis_size("dp") * lax.axis_size("mp")
    return lax.ppermute(x, ("dp", "mp"), [(i, i ^ (second if i % 2 else first)) for i in range(n)])


def turned(steps, by):
    return steps[by:] + steps[:by]


def butterfly(halves, orders, first, last):
    for i in range(first, last):
        got = [pairwise(halves[h], orders[2 * h][i], orders[2 * h + 1][i]) for h in (0, 1)]
        halves = [mine + other for mine, other in zip(halves, got)]
    return halves


def body(grad_flat, error_flat, momentum_flat, warm_x, warm_b, warm_c, warm_dt, part_order):
    blocks = lax.axis_size("mp")
    replicas = lax.axis_size("dp")
    plan = Plan(blocks)
    rows = plan.rows
    total = plan.total
    shape = jax.ShapeDtypeStruct
    pieces = len(plan.pieces)
    dma = pltpu.SemaphoreType.DMA
    top, low, mh, ml, m = pl.pallas_call(
        functools.partial(panel_kernel, plan),
        out_shape=(
            shape((plan.half, LANES), f32),
            shape((plan.panel_rows - plan.half, LANES), f32),
            shape((rows, COLS), bf16),
            shape((rows, COLS), bf16),
            shape((plan.buf_rows, LANES), f32),
        ),
        in_specs=specs(*[HBM] * 7),
        out_specs=tuple(specs(*[VMEM] * 5)),
        scratch_shapes=[
            pltpu.SMEM((6,), jnp.int32),
            pltpu.VMEM((1, total), bf16),
            pltpu.VMEM((1, total), bf16),
            pltpu.VMEM((RANK, DI), f32),
            pltpu.VMEM((RANK, DS), f32),
            pltpu.VMEM((RANK, DS), f32),
            pltpu.VMEM((RANK, NH), f32),
            pltpu.VMEM((rows, LANES), f32),
            pltpu.VMEM((RANK, LANES), f32),
            dma((5 + 2 * pieces,)),
        ],
        compiler_params=pltpu.CompilerParams(vmem_limit_bytes=36 << 20),
        cost_estimate=pl.CostEstimate(flops=4 * rows * COLS * LANES, bytes_accessed=8 * total, transcendentals=0),
    )(*(pltpu.with_memory_space_constraint(x, HBM) for x in (part_order, grad_flat, error_flat, warm_x.T, warm_b.T, warm_c.T, warm_dt.T)))

    inner = [1 << b for b in range(1, (blocks - 1).bit_length())]
    outer = [blocks << b for b in range((replicas - 1).bit_length())]
    orders = [outer, turned(outer, len(outer) - 1), turned(outer, 1), outer]
    top, low = butterfly([top, low], orders, 0, len(outer))
    outer = outer[1:2] + outer[:1] + outer[2:]

    quarter, half = RANK // 4, RANK // 2
    mine0, mine1, other = pl.pallas_call(
        functools.partial(factor_kernel, plan),
        out_shape=(shape((quarter, WITH_GRAM), f32), shape((quarter, COLS), f32), shape((half, WITH_GRAM), f32)),
        in_specs=specs(*[VMEM] * 4),
        out_specs=tuple(specs(*[VMEM] * 3)),
        scratch_shapes=[pltpu.VMEM((RANK, COLS), f32)],
        compiler_params=pltpu.CompilerParams(vmem_limit_bytes=24 << 20),
        cost_estimate=pl.CostEstimate(flops=4 * rows * COLS * LANES, bytes_accessed=4 * total, transcendentals=0),
    )(top, low, mh, ml)
    got = pairwise(other, 1, 1)
    halves = [mine0 + got[:quarter], mine1 + got[quarter:, :COLS]]
    square = shape((LANES, LANES), f32)

    def begin(gram):
        return pl.pallas_call(
            begin_kernel,
            out_shape=(square, square, shape((8, LANES), f32)),
            in_specs=specs(VMEM),
            out_specs=tuple(specs(*[VMEM] * 3)),
            compiler_params=pltpu.CompilerParams(vmem_limit_bytes=4 << 20),
            cost_estimate=pl.CostEstimate(flops=1500000000, bytes_accessed=200000, transcendentals=0),
        )(gram)

    def frame(made):
        return pl.pallas_call(
            functools.partial(frame_kernel, plan, replicas),
            out_shape=shape((4 * rows, LANES), bf16),
            in_specs=specs(*[VMEM] * 5),
            out_specs=specs(VMEM)[0],
            compiler_params=pltpu.CompilerParams(vmem_limit_bytes=8 << 20),
            cost_estimate=pl.CostEstimate(flops=1500000000, bytes_accessed=600000, transcendentals=0),
        )(*made, top, low)

    gram, halves[0] = halves[0][:, COLS:], halves[0][:, :COLS]
    for bit in inner:
        gram = gram + pairwise(gram, bit, bit)
    ring = inner + outer
    n = len(ring)
    orders = [turned(ring, by) for by in (0, n // 2, 1, 1 + n // 2)]
    halves = butterfly(halves, orders, 0, 1)
    halves[0], gram = lax.optimization_barrier((halves[0], gram))
    halves = butterfly(halves, orders, 1, 2)
    halves[1], gram = lax.optimization_barrier((halves[1], gram))
    halves = butterfly(halves, orders, 2, 3)
    made = begin(gram)
    halves[0], made = lax.optimization_barrier((halves[0], made))
    lhs = frame(made)
    halves = butterfly(halves, orders, 3, n)
    halves[0], lhs = lax.optimization_barrier((halves[0], lhs))
    halves[1], lhs = lax.optimization_barrier((halves[1], lhs))
    others = [pairwise(half, 1, 1) for half in halves]

    return pl.pallas_call(
        functools.partial(output_kernel, plan, replicas),
        out_shape=(shape((1, total), bf16), shape((total,), f32)),
        in_specs=specs(pltpu.SMEM, *[VMEM] * 8),
        out_specs=tuple(specs(HBM, HBM)),
        scratch_shapes=[
            pltpu.VMEM((RANK, COLS), f32),
            pltpu.VMEM((plan.buf_rows, LANES), f32),
            pltpu.VMEM((rows + 8, COLS), f32),
            pltpu.VMEM((rows + 24, LANES), f32),
            pltpu.VMEM((1, total), bf16),
            pltpu.VMEM((total,), f32),
            dma((2 * pieces,)),
        ],
        compiler_params=pltpu.CompilerParams(vmem_limit_bytes=36 << 20),
        cost_estimate=pl.CostEstimate(flops=2 * rows * COLS * LANES, bytes_accessed=16 * total, transcendentals=0),
    )(part_order, *halves, *others, lhs, low, m, momentum_flat)


def solution(mesh):
    placed = (P("dp", "mp"), P("dp", "mp"), P("mp"), P(), P(), P(), P(), P())
    return jax.shard_map(
        body, mesh=mesh, in_specs=placed, out_specs=(P("dp", "mp"), P("mp")), check_vma=False
    )
```

```python
import functools

import jax
import jax.numpy as jnp
from jax import lax
from jax.experimental import pallas as pl
from jax.experimental.pallas import tpu as pltpu
from jax.sharding import PartitionSpec as P

D = 1536
DI = 3072
DS = 128
NH = 48
KW = 4
RANK = 32
NS_STEPS = 5
CONV_CH = 3328
VEC = 3472
LANES = 128

momentum_decay = 0.9
ns_first = 3.4445
ns_second = -4.775
ns_third = 2.0315

COL_B = DI
COL_C = DI + DS
COL_DT = DI + 2 * DS
COLS = DI + 3 * DS
WITH_GRAM = COLS + 4 * LANES
CHUNKS = DI // LANES

MERGE = 256
FINISH = 128
PIECES = 8

f32 = jnp.float32
bf16 = jnp.bfloat16
HBM = pltpu.MemorySpace.HBM
VMEM = pltpu.MemorySpace.VMEM


class Plan:
    def __init__(self, blocks):
        self.rows = D // blocks
        self.sizes = [
            D * DI // blocks,
            D * DS // blocks,
            D * DS // blocks,
            D * NH // blocks,
            CONV_CH * KW // blocks,
            VEC // blocks,
        ]
        self.total = sum(self.sizes)
        self.flat_rows = -(-self.total // LANES)
        self.buf_rows = (self.flat_rows + 15) // 8 * 8 + 16
        self.dt_groups = self.rows // 8
        self.conv_rows = self.sizes[4] // LANES
        self.conv_pad = -(-self.conv_rows // 8) * 8
        self.vec_rows = -(-self.sizes[5] // LANES)
        self.vec_pad = -(-self.vec_rows // 8) * 8
        self.panel_rows = self.rows + self.conv_pad + self.vec_pad
        self.shift = self.sizes[5] % LANES
        self.half = -(-self.panel_rows // 16) * 8
        step = -(-self.flat_rows // (PIECES * MERGE)) * MERGE
        cuts = list(range(0, self.flat_rows, step)) + [self.flat_rows]
        self.pieces = list(zip(cuts, cuts[1:]))


def starts_of(order_ref, sizes):
    zero = jnp.int32(0)
    first = [zero] * 6
    run = zero
    for place in range(6):
        part = order_ref[place]
        size = zero
        for k in range(6):
            here = part == k
            first[k] = jnp.where(here, run, first[k])
            size = jnp.where(here, jnp.int32(sizes[k]), size)
        run = run + size
    return [lax.shift_right_logical(o, 7) for o in first], [jnp.bitwise_and(o, 127) for o in first]


def lane_of(shape):
    return lax.broadcasted_iota(jnp.int32, shape, len(shape) - 1)


def split2(x):
    hi = x.astype(bf16)
    return hi, (x - hi.astype(f32)).astype(bf16)


def split3(x):
    hi = x.astype(bf16)
    rest = x - hi.astype(f32)
    mid = rest.astype(bf16)
    return hi, mid, (rest - mid.astype(f32)).astype(bf16)


def dot_nt(a, b):
    return lax.dot_general(a, b, (((1,), (1,)), ((), ())), preferred_element_type=f32)


def dot_tn(a, b):
    return lax.dot_general(a, b, (((0,), (0,)), ((), ())), preferred_element_type=f32)


def dot_exact(a, b):
    return lax.dot_general(
        a, b, (((1,), (0,)), ((), ())), preferred_element_type=f32, precision=lax.Precision.HIGHEST
    )


def spread(x, group):
    x = jnp.where(lane_of(x.shape) // RANK == group, x, 0.0)
    x = x + pltpu.roll(x, 64, 1)
    return x + pltpu.roll(x, 32, 1)


def panel_kernel(plan, order_hbm, g_hbm, e_hbm, wx_hbm, wb_hbm, wc_hbm, wd_hbm, top_ref, low_ref, mh_ref, ml_ref, m_ref, order_ref, g_ref, e_ref, wx_ref, wb_ref, wc_ref, wd_ref, dt_ref, w_ref, sems):
    rows = plan.rows
    total = plan.total
    shift = plan.shift

    small = [
        pltpu.make_async_copy(src, dst, sems.at[i])
        for i, (src, dst) in enumerate(
            ((order_hbm, order_ref), (wx_hbm, wx_ref), (wb_hbm, wb_ref), (wc_hbm, wc_ref), (wd_hbm, wd_ref))
        )
    ]
    big = []
    for i, (begin, end) in enumerate(plan.pieces):
        part = (slice(0, 1), slice(begin * LANES, min(end * LANES, total)))
        big.append(
            [
                pltpu.make_async_copy(src.at[part], dst.at[part], sems.at[5 + 2 * i + j])
                for j, (src, dst) in enumerate(((g_hbm, g_ref), (e_hbm, e_ref)))
            ]
        )
    small[0].start()
    for i, pair in enumerate(big):
        for copy in pair:
            copy.start()
        if i == 0:
            for copy in small[1:]:
                copy.start()
    small[0].wait()
    row, lane = starts_of(order_ref, plan.sizes)

    def merged(at, width):
        return g_ref[0:1, pl.ds(at, width)].astype(f32) + e_ref[0:1, pl.ds(at, width)].astype(f32)

    def fetch(base, count, stride, moved):
        step = {} if stride == 1 else {"stride": stride}
        now = m_ref[pl.ds(base, count, **step), :]
        return pltpu.roll(now, LANES - shift, 1) if moved else now

    def joined(base, count, stride, moved):
        now = fetch(base, count, stride, moved)
        if not moved:
            return now
        return jnp.where(lane_of((count, LANES)) < LANES - shift, now, fetch(base + 1, count, stride, moved))

    def either(k, work):
        for moved in (False, True):
            pl.when((lane[k] != 0) == moved)(functools.partial(work, moved))

    def put(at, count, column, tile):
        hi, lo = split2(tile)
        mh_ref[pl.ds(at, count), column : column + LANES] = hi
        ml_ref[pl.ds(at, count), column : column + LANES] = lo

    high = 32

    def read_x(first, last, moved):
        keep = lane_of((high, LANES)) < LANES - shift

        def block(i, _):
            base = row[0] + i * (high * CHUNKS)
            at = pl.multiple_of(i * high, high)
            now = fetch(base, high, CHUNKS, moved)
            for c in range(CHUNKS):
                tile = now
                if moved or c + 1 < CHUNKS:
                    now = fetch(base + (c + 1), high, CHUNKS, moved)
                if moved:
                    tile = jnp.where(keep, tile, now)
                put(at, high, c * LANES, tile)
            return 0

        lax.fori_loop(first, last, block, 0)

    done = 0
    for (begin, end), pair in zip(plan.pieces, big):
        for copy in pair:
            copy.wait()
        whole = min(end, total // LANES)

        def merge(i, _):
            r = pl.multiple_of(begin + i * MERGE, 8)
            m_ref[pl.ds(r, MERGE), :] = merged(pl.multiple_of(r * LANES, 1024), MERGE * LANES).reshape(MERGE, LANES)
            return 0

        count = (whole - begin) // MERGE
        lax.fori_loop(0, count, merge, 0)
        r = begin + count * MERGE
        n = (whole - r) // 8 * 8
        if n:
            m_ref[r : r + n, :] = merged(r * LANES, n * LANES).reshape(n, LANES)
        for r in range(r + n, whole):
            m_ref[r : r + 1, :] = merged(LANES * r, LANES)
        if end > whole:
            m_ref[whole : whole + 1, 0 : total % LANES] = merged(LANES * whole, total % LANES)

        ready = rows // high
        if end < plan.flat_rows:
            ready = jnp.minimum(lax.div(jnp.maximum(end - 1 - row[0], 0), jnp.int32(high * CHUNKS)), rows // high)
        either(0, functools.partial(read_x, done, ready))
        done = ready
    for copy in small[1:]:
        copy.wait()
    for k, column in ((1, COL_B), (2, COL_C)):
        either(k, lambda moved, k=k, column=column: put(0, rows, column, joined(row[k], rows, 1, moved)))

    groups = plan.dt_groups
    lanes_dt = lane_of((groups, LANES))

    def read_dt(moved):
        thirds = [joined(row[3] + q, groups, 3, moved) for q in range(3)]
        for b in range(8):
            q, s = divmod(NH * b, LANES)
            piece = thirds[q] if s == 0 else pltpu.roll(thirds[q], LANES - s, 1)
            if s + NH > LANES:
                piece = jnp.where(lanes_dt < LANES - s, piece, pltpu.roll(thirds[q + 1], LANES - s, 1))
            dt_ref[b * groups : (b + 1) * groups, :] = jnp.where(lanes_dt < NH, piece, 0.0)

    either(3, read_dt)
    put(0, rows, COL_DT, dt_ref[...])

    low = rows - plan.half

    def read_conv(moved):
        shape = (plan.conv_pad, LANES)
        conv = joined(row[4], plan.conv_pad, 1, moved)
        conv = jnp.where(lax.broadcasted_iota(jnp.int32, shape, 0) < plan.conv_rows, conv, 0.0)
        low_ref[low : low + plan.conv_pad, :] = conv

    either(4, read_conv)
    shape = (plan.vec_pad, LANES)
    place = lax.broadcasted_iota(jnp.int32, shape, 0) * LANES + lane_of(shape)
    vec = jnp.where(place < plan.sizes[5], m_ref[pl.ds(row[5], plan.vec_pad), :], 0.0)
    low_ref[low + plan.conv_pad :, :] = vec

    w_ref[...] = jnp.zeros_like(w_ref)
    w_ref[:, 0:NH] = wd_ref[...]
    panel = None
    lanes = lane_of((rows, LANES))
    for k, (w, column, width) in enumerate(
        ((wx_ref, 0, DI), (wb_ref, COL_B, DS), (wc_ref, COL_C, DS), (w_ref, COL_DT, LANES))
    ):
        hi, mid, lo = split3(w[...])
        none = jnp.zeros_like(hi)
        part = dot_nt(mh_ref[:, column : column + width], jnp.concatenate([hi, mid, lo, none], 0))
        part = part + dot_nt(ml_ref[:, column : column + width], jnp.concatenate([hi, mid, none, none], 0))
        part = part + pltpu.roll(part, 64, 1)
        part = part + pltpu.roll(part, 32, 1)
        panel = part if k == 0 else jnp.where(lanes >= RANK * k, part, panel)
    top_ref[...] = panel[0 : plan.half]
    low_ref[0:low, :] = panel[plan.half :]


def factor_kernel(plan, top_ref, low_ref, mh_ref, ml_ref, mine0_ref, mine1_ref, other_ref, z_ref):
    rows = plan.rows
    panel = jnp.concatenate([top_ref[...], low_ref[0 : rows - plan.half, :]], 0)
    group = lane_of((rows, LANES)) // RANK
    for k, column, width in ((0, 0, DI), (1, COL_B, DS), (2, COL_C, DS), (3, COL_DT, DS)):
        hi, mid, lo = (piece.astype(f32) for piece in split3(spread(panel, k)))
        two = jnp.where(group == 0, hi, jnp.where(group == 1, mid, 0.0))
        three = jnp.where(group == 2, lo, two).astype(bf16)
        two = two.astype(bf16)
        z = dot_tn(three, mh_ref[:, column : column + width]) + dot_tn(two, ml_ref[:, column : column + width])
        z_ref[:, column : column + width] = z[0:32] + z[32:64] + z[64:96]
    gram = lax.dot_general(
        panel, panel, (((0,), (0,)), ((), ())), preferred_element_type=f32, precision=lax.Precision.HIGHEST
    )
    group = lane_of((RANK, LANES)) // RANK
    out = gram[0:RANK]
    for k in range(1, 4):
        out = jnp.where(group == k, gram[RANK * k : RANK * (k + 1)], out)
    half = RANK // 2
    core = jnp.bitwise_and(lax.axis_index("mp"), 1)
    for mine in (0, 1):

        @pl.when(core == mine)
        def _():
            mine0_ref[:, 0:COLS] = z_ref[half * mine : half * mine + half // 2, :]
            mine1_ref[...] = z_ref[half * mine + half // 2 : half * (mine + 1), :]
            other_ref[:, 0:COLS] = z_ref[half * (1 - mine) : half * (2 - mine), :]

    other_ref[:, COLS:] = jnp.zeros((half, 4 * LANES), f32)
    for b in range(4):
        lanes = slice(COLS + b * LANES, COLS + (b + 1) * LANES)
        mine0_ref[:, lanes] = out[8 * b : 8 * (b + 1)]
        other_ref[0:8, lanes] = out[8 * b : 8 * (b + 1)]


def block_masks():
    square = (LANES, LANES)
    down = lax.broadcasted_iota(jnp.int32, square, 0)
    along = lane_of(square)
    return jnp.where(down == along, 1.0, 0.0), jnp.where(down // RANK == along // RANK, 1.0, 0.0)


def newton_schulz(eye, gram, turned, steps, last):
    for step in range(steps):
        mixing = ns_first * eye + ns_second * gram + ns_third * dot_exact(gram, gram)
        turned = mixing if turned is None else dot_exact(turned, mixing)
        if not (last and step + 1 == steps):
            gram = dot_exact(mixing, dot_exact(gram, mixing))
    return gram, turned


def begin_kernel(sum_ref, gram_out, turned_out, scale_out):
    eye, ones = block_masks()
    gram = [sum_ref[:, b * LANES : (b + 1) * LANES] for b in range(4)]
    gram = jnp.concatenate(gram * 4, 0) * ones
    trace = jnp.sum(gram * eye, axis=0, keepdims=True)
    trace = dot_exact(jnp.broadcast_to(trace, (8, LANES)), ones)
    scale = 1.0 / (jnp.sqrt(trace) + 1e-06)
    scale = scale * scale
    scale_out[...] = scale
    gram_out[...], turned_out[...] = newton_schulz(eye, gram * scale[0:1], None, NS_STEPS // 2, False)


def frame_kernel(plan, replicas, gram_ref, turned_ref, scale_ref, top_ref, low_ref, lhs_ref):
    rows = plan.rows
    eye, _ = block_masks()
    _, turned = newton_schulz(eye, gram_ref[...], turned_ref[...], NS_STEPS - NS_STEPS // 2, True)
    both = lax.dot_general(
        turned, turned, (((1,), (1,)), ((), ())), preferred_element_type=f32, precision=lax.Precision.HIGHEST
    )
    panel = jnp.concatenate([top_ref[...], low_ref[0 : rows - plan.half, :]], 0)
    left = dot_exact(panel, both * (scale_ref[0:1] * (1.0 / replicas)))
    group = lane_of((rows, LANES)) // RANK
    for k in range(4):
        hi, mid = (piece.astype(f32) for piece in split2(spread(left, k)))
        lhs_ref[k * rows : (k + 1) * rows, :] = jnp.where(group % 2 == 0, hi, mid).astype(bf16)


def output_kernel(plan, replicas, order_ref, mine0_ref, mine1_ref, other0_ref, other1_ref, lhs_ref, low_ref, m_ref, mom_ref, err_hbm, next_hbm, z_ref, t_ref, a_ref, x_ref, s_ref, err_ref, next_ref, sems):
    rows = plan.rows
    shift = plan.shift
    row, lane = starts_of(order_ref, plan.sizes)

    quarter = RANK // 4
    core = jnp.bitwise_and(lax.axis_index("mp"), 1)
    for mine in (0, 1):

        @pl.when(core == mine)
        def _():
            for i, ref in enumerate((mine0_ref, mine1_ref, other0_ref, other1_ref)):
                at = (2 * mine + i) % 4 * quarter
                z_ref[at : at + quarter, :] = ref[...]

    @pl.when(lane[0] != 0)
    def _():
        keep = lane_of((RANK, LANES)) >= shift
        before = jnp.zeros((RANK, LANES), f32)
        for c in range(CHUNKS):
            columns = slice(c * LANES, (c + 1) * LANES)
            now = pltpu.roll(z_ref[:, columns], shift, 1)
            z_ref[:, columns] = jnp.where(keep, now, before)
            before = now
        t_ref[...] = before

    def product(k, factor):
        hi, mid = split2(factor)
        return jnp.dot(
            lhs_ref[k * rows : (k + 1) * rows, :],
            jnp.concatenate([hi, hi, mid, mid], 0),
            preferred_element_type=f32,
        )

    for k, column, width in ((0, 0, DI), (1, COL_B, DS), (2, COL_C, DS), (3, COL_DT, DS)):
        x_ref[8 : 8 + rows, column : column + width] = product(k, z_ref[:, column : column + width])

    high = 32
    lanes1 = lane_of((1, LANES))

    def right(x):
        return pltpu.roll(x, shift, 1)

    def either(k, work):
        for moved in (False, True):
            pl.when((lane[k] != 0) == moved)(functools.partial(work, moved))

    def write_x(first, last, moved):
        keep = lane_of((high, LANES)) >= shift

        def block(i, _):
            at = pl.multiple_of(8 + i * high, 8)
            base = row[0] + i * (high * CHUNKS)
            for c in range(CHUNKS):
                now = x_ref[pl.ds(at, high), c * LANES : (c + 1) * LANES]
                if moved and c == 0:
                    now = jnp.where(keep, now, s_ref[pl.ds(at - 1, high), :])
                a_ref[pl.ds(base + c, high, stride=CHUNKS), :] = now
            return 0

        lax.fori_loop(first, last, block, 0)


    def place(k, ref, column, count):
        columns = slice(column, column + LANES)

        def work(moved):
            if not moved:
                a_ref[pl.ds(row[k], count), :] = ref[8 : 8 + count, columns]
                return
            head = right(ref[8:16, columns])[0:1]
            end = right(ref[count : count + 8, columns])[7:8]
            a_ref[pl.ds(row[k], 1), :] = jnp.where(lanes1 >= shift, head, a_ref[pl.ds(row[k], 1), :])
            final = row[k] + count
            a_ref[pl.ds(final, 1), :] = jnp.where(lanes1 < shift, end, a_ref[pl.ds(final, 1), :])
            n = count - 1
            now = right(ref[9 : 9 + n, columns])
            before = right(ref[8 : 8 + n, columns])
            a_ref[pl.ds(row[k] + 1, n), :] = jnp.where(lane_of((n, LANES)) >= shift, now, before)

        either(k, work)

    place(1, x_ref, COL_B, rows)
    place(2, x_ref, COL_C, rows)
    groups = plan.dt_groups
    lanes_dt = lane_of((groups, LANES))
    for q in range(3):
        third = jnp.zeros((groups, LANES), f32)
        for b in range(8):
            lo = NH * b - LANES * q
            if lo <= -NH or lo >= LANES:
                continue
            piece = x_ref[8 + b * groups : 8 + (b + 1) * groups, COL_DT : COL_DT + LANES]
            if lo % LANES:
                piece = pltpu.roll(piece, lo % LANES, 1)
            third = jnp.where((lanes_dt >= lo) & (lanes_dt < lo + NH), piece, third)
        s_ref[pl.ds(8 + q, groups, stride=3), :] = third
    place(3, s_ref, 0, 3 * groups)
    low = rows - plan.half
    s_ref[8 : 8 + plan.conv_pad, :] = low_ref[low : low + plan.conv_pad, :] * (1.0 / replicas)
    place(4, s_ref, 0, plan.conv_rows)
    vec = low_ref[low + plan.conv_pad :, :] * (1.0 / replicas)
    last = plan.vec_rows - 1
    a_ref[pl.ds(row[5], last), :] = vec[0:last]
    final = row[5] + last
    valid = plan.sizes[5] - last * LANES
    a_ref[pl.ds(final, 1), :] = jnp.where(lanes1 < valid, vec[last : last + 1], a_ref[pl.ds(final, 1), :])

    @pl.when(lane[0] != 0)
    def _():
        s_ref[8 : 8 + rows, :] = product(0, t_ref[...])
        s_ref[7:8, :] = a_ref[pl.ds(row[0], 1), :]
        final = row[0] + rows * CHUNKS
        end = s_ref[rows + 7 : rows + 8, :]
        a_ref[pl.ds(final, 1), :] = jnp.where(lanes1 < shift, end, a_ref[pl.ds(final, 1), :])

    total = plan.total
    spans = [(row[k] * LANES + lane[k], row[k] * LANES + lane[k] + plan.sizes[k]) for k in (4, 5)]

    def finish(at_row, count, width=LANES):
        n = count * width
        at = at_row * LANES
        a = a_ref[pl.ds(at_row, count), 0:width]
        next_ref[pl.ds(at, n)] = momentum_decay * mom_ref[pl.ds(at, n)] + a.reshape(n)
        near = [(at < end) & (at + n > begin) for begin, end in spans]
        near = near[0] | near[1]

        @pl.when(jnp.logical_not(near))
        def _():
            err = m_ref[pl.ds(at_row, count), 0:width] - a_ref[pl.ds(at_row, count), 0:width]
            err_ref[0:1, pl.ds(at, n)] = err.astype(bf16).reshape(1, n)

        @pl.when(near)
        def _():
            err = m_ref[pl.ds(at_row, count), 0:width] - a_ref[pl.ds(at_row, count), 0:width]
            index = lax.broadcasted_iota(jnp.int32, err.shape, 0) * LANES + lane_of(err.shape) + at
            for begin, end in spans:
                err = jnp.where((index >= begin) & (index < end), 0.0, err)
            err_ref[0:1, pl.ds(at, n)] = err.astype(bf16).reshape(1, n)

    copies = []
    done = 0
    for i, (begin, end) in enumerate(plan.pieces):
        step = high * CHUNKS
        ready = rows // high
        if end < plan.flat_rows:
            ready = jnp.minimum(lax.div(jnp.maximum(end - row[0], 0) + (step - 1), jnp.int32(step)), rows // high)
        either(0, functools.partial(write_x, done, ready))
        done = ready
        whole = min(end, total // LANES)
        count = (whole - begin) // FINISH
        lax.fori_loop(0, count, lambda j, _: (finish(pl.multiple_of(begin + j * FINISH, 8), FINISH), 0)[1], 0)
        r = begin + count * FINISH
        n = (whole - r) // 8 * 8
        if n:
            finish(r, n)
        for r in range(r + n, whole):
            finish(r, 1)
        if end > whole:
            finish(whole, 1, total % LANES)
        part = slice(begin * LANES, min(end * LANES, total))
        copies.append(pltpu.make_async_copy(err_ref.at[0:1, part], err_hbm.at[0:1, part], sems.at[2 * i]))
        copies.append(pltpu.make_async_copy(next_ref.at[part], next_hbm.at[part], sems.at[2 * i + 1]))
        for copy in copies[-2:]:
            copy.start()
    for copy in copies:
        copy.wait()


def specs(*spaces):
    return [pl.BlockSpec(memory_space=space) for space in spaces]


def pairwise(x, first, second):
    n = lax.axis_size("dp") * lax.axis_size("mp")
    return lax.ppermute(x, ("dp", "mp"), [(i, i ^ (second if i % 2 else first)) for i in range(n)])


def turned(steps, by):
    return steps[by:] + steps[:by]


def butterfly(halves, orders, first, last):
    for i in range(first, last):
        got = [pairwise(halves[h], orders[2 * h][i], orders[2 * h + 1][i]) for h in (0, 1)]
        halves = [mine + other for mine, other in zip(halves, got)]
    return halves


def body(grad_flat, error_flat, momentum_flat, warm_x, warm_b, warm_c, warm_dt, part_order):
    blocks = lax.axis_size("mp")
    replicas = lax.axis_size("dp")
    plan = Plan(blocks)
    rows = plan.rows
    total = plan.total
    shape = jax.ShapeDtypeStruct
    pieces = len(plan.pieces)
    dma = pltpu.SemaphoreType.DMA
    top, low, mh, ml, m = pl.pallas_call(
        functools.partial(panel_kernel, plan),
        out_shape=(
            shape((plan.half, LANES), f32),
            shape((plan.panel_rows - plan.half, LANES), f32),
            shape((rows, COLS), bf16),
            shape((rows, COLS), bf16),
            shape((plan.buf_rows, LANES), f32),
        ),
        in_specs=specs(*[HBM] * 7),
        out_specs=tuple(specs(*[VMEM] * 5)),
        scratch_shapes=[
            pltpu.SMEM((6,), jnp.int32),
            pltpu.VMEM((1, total), bf16),
            pltpu.VMEM((1, total), bf16),
            pltpu.VMEM((RANK, DI), f32),
            pltpu.VMEM((RANK, DS), f32),
            pltpu.VMEM((RANK, DS), f32),
            pltpu.VMEM((RANK, NH), f32),
            pltpu.VMEM((rows, LANES), f32),
            pltpu.VMEM((RANK, LANES), f32),
            dma((5 + 2 * pieces,)),
        ],
        compiler_params=pltpu.CompilerParams(vmem_limit_bytes=36 << 20),
        cost_estimate=pl.CostEstimate(flops=4 * rows * COLS * LANES, bytes_accessed=8 * total, transcendentals=0),
    )(*(pltpu.with_memory_space_constraint(x, HBM) for x in (part_order, grad_flat, error_flat, warm_x.T, warm_b.T, warm_c.T, warm_dt.T)))

    inner = [1 << b for b in range(1, (blocks - 1).bit_length())]
    outer = [blocks << b for b in range((replicas - 1).bit_length())]
    orders = [outer, turned(outer, len(outer) - 1), turned(outer, 1), outer]
    top, low = butterfly([top, low], orders, 0, len(outer))
    outer = outer[1:2] + outer[:1] + outer[2:]

    quarter, half = RANK // 4, RANK // 2
    mine0, mine1, other = pl.pallas_call(
        functools.partial(factor_kernel, plan),
        out_shape=(shape((quarter, WITH_GRAM), f32), shape((quarter, COLS), f32), shape((half, WITH_GRAM), f32)),
        in_specs=specs(*[VMEM] * 4),
        out_specs=tuple(specs(*[VMEM] * 3)),
        scratch_shapes=[pltpu.VMEM((RANK, COLS), f32)],
        compiler_params=pltpu.CompilerParams(vmem_limit_bytes=24 << 20),
        cost_estimate=pl.CostEstimate(flops=4 * rows * COLS * LANES, bytes_accessed=4 * total, transcendentals=0),
    )(top, low, mh, ml)
    got = pairwise(other, 1, 1)
    halves = [mine0 + got[:quarter], mine1 + got[quarter:, :COLS]]
    square = shape((LANES, LANES), f32)

    def begin(gram):
        return pl.pallas_call(
            begin_kernel,
            out_shape=(square, square, shape((8, LANES), f32)),
            in_specs=specs(VMEM),
            out_specs=tuple(specs(*[VMEM] * 3)),
            compiler_params=pltpu.CompilerParams(vmem_limit_bytes=4 << 20),
            cost_estimate=pl.CostEstimate(flops=1500000000, bytes_accessed=200000, transcendentals=0),
        )(gram)

    def frame(made):
        return pl.pallas_call(
            functools.partial(frame_kernel, plan, replicas),
            out_shape=shape((4 * rows, LANES), bf16),
            in_specs=specs(*[VMEM] * 5),
            out_specs=specs(VMEM)[0],
            compiler_params=pltpu.CompilerParams(vmem_limit_bytes=8 << 20),
            cost_estimate=pl.CostEstimate(flops=1500000000, bytes_accessed=600000, transcendentals=0),
        )(*made, top, low)

    gram, halves[0] = halves[0][:, COLS:], halves[0][:, :COLS]
    ring = inner + outer
    n = len(ring)
    orders = [turned(ring, by) for by in (0, n // 2, 1, 1 + n // 2)]
    halves = butterfly(halves, orders, 0, 1)
    halves[0], gram = lax.optimization_barrier((halves[0], gram))
    for bit in inner:
        gram = gram + pairwise(gram, bit, bit)
    halves = butterfly(halves, orders, 1, 2)
    halves[1], gram = lax.optimization_barrier((halves[1], gram))
    halves = butterfly(halves, orders, 2, 3)
    made = begin(gram)
    halves[0], made = lax.optimization_barrier((halves[0], made))
    lhs = frame(made)
    halves = butterfly(halves, orders, 3, n)
    halves[0], lhs = lax.optimization_barrier((halves[0], lhs))
    halves[1], lhs = lax.optimization_barrier((halves[1], lhs))
    others = [pairwise(half, 1, 1) for half in halves]

    return pl.pallas_call(
        functools.partial(output_kernel, plan, replicas),
        out_shape=(shape((1, total), bf16), shape((total,), f32)),
        in_specs=specs(pltpu.SMEM, *[VMEM] * 8),
        out_specs=tuple(specs(HBM, HBM)),
        scratch_shapes=[
            pltpu.VMEM((RANK, COLS), f32),
            pltpu.VMEM((RANK, LANES), f32),
            pltpu.VMEM((plan.buf_rows, LANES), f32),
            pltpu.VMEM((rows + 8, COLS), f32),
            pltpu.VMEM((rows + 24, LANES), f32),
            pltpu.VMEM((1, total), bf16),
            pltpu.VMEM((total,), f32),
            dma((2 * pieces,)),
        ],
        compiler_params=pltpu.CompilerParams(vmem_limit_bytes=36 << 20),
        cost_estimate=pl.CostEstimate(flops=2 * rows * COLS * LANES, bytes_accessed=16 * total, transcendentals=0),
    )(part_order, *halves, *others, lhs, low, m, momentum_flat)


def solution(mesh):
    placed = (P("dp", "mp"), P("dp", "mp"), P("mp"), P(), P(), P(), P(), P())
    return jax.shard_map(
        body, mesh=mesh, in_specs=placed, out_specs=(P("dp", "mp"), P("mp")), check_vma=False
    )
```

```python
import functools

import jax
import jax.numpy as jnp
from jax import lax
from jax.experimental import pallas as pl
from jax.experimental.pallas import tpu as pltpu
from jax.sharding import PartitionSpec as P

D = 1536
DI = 3072
DS = 128
NH = 48
KW = 4
RANK = 32
NS_STEPS = 5
CONV_CH = 3328
VEC = 3472
LANES = 128

momentum_decay = 0.9
ns_first = 3.4445
ns_second = -4.775
ns_third = 2.0315

COL_B = DI
COL_C = DI + DS
COL_DT = DI + 2 * DS
COLS = DI + 3 * DS
WITH_GRAM = COLS + 4 * LANES
CHUNKS = DI // LANES

MERGE = 256
FINISH = 256
PIECES = 8

f32 = jnp.float32
bf16 = jnp.bfloat16
HBM = pltpu.MemorySpace.HBM
VMEM = pltpu.MemorySpace.VMEM


class Plan:
    def __init__(self, blocks):
        self.rows = D // blocks
        self.sizes = [
            D * DI // blocks,
            D * DS // blocks,
            D * DS // blocks,
            D * NH // blocks,
            CONV_CH * KW // blocks,
            VEC // blocks,
        ]
        self.total = sum(self.sizes)
        self.flat_rows = -(-self.total // LANES)
        self.buf_rows = (self.flat_rows + 15) // 8 * 8 + 16
        self.dt_groups = self.rows // 8
        self.conv_rows = self.sizes[4] // LANES
        self.conv_pad = -(-self.conv_rows // 8) * 8
        self.vec_rows = -(-self.sizes[5] // LANES)
        self.vec_pad = -(-self.vec_rows // 8) * 8
        self.panel_rows = self.rows + self.conv_pad + self.vec_pad
        self.shift = self.sizes[5] % LANES
        self.half = -(-self.panel_rows // 16) * 8
        step = -(-self.flat_rows // (PIECES * MERGE)) * MERGE
        cuts = list(range(0, self.flat_rows, step)) + [self.flat_rows]
        self.pieces = list(zip(cuts, cuts[1:]))


def starts_of(order_ref, sizes):
    zero = jnp.int32(0)
    first = [zero] * 6
    run = zero
    for place in range(6):
        part = order_ref[place]
        size = zero
        for k in range(6):
            here = part == k
            first[k] = jnp.where(here, run, first[k])
            size = jnp.where(here, jnp.int32(sizes[k]), size)
        run = run + size
    return [lax.shift_right_logical(o, 7) for o in first], [jnp.bitwise_and(o, 127) for o in first]


def lane_of(shape):
    return lax.broadcasted_iota(jnp.int32, shape, len(shape) - 1)


def split2(x):
    hi = x.astype(bf16)
    return hi, (x - hi.astype(f32)).astype(bf16)


def split3(x):
    hi = x.astype(bf16)
    rest = x - hi.astype(f32)
    mid = rest.astype(bf16)
    return hi, mid, (rest - mid.astype(f32)).astype(bf16)


def dot_nt(a, b):
    return lax.dot_general(a, b, (((1,), (1,)), ((), ())), preferred_element_type=f32)


def dot_tn(a, b):
    return lax.dot_general(a, b, (((0,), (0,)), ((), ())), preferred_element_type=f32)


def dot_exact(a, b):
    return lax.dot_general(
        a, b, (((1,), (0,)), ((), ())), preferred_element_type=f32, precision=lax.Precision.HIGHEST
    )


def spread(x, group):
    x = jnp.where(lane_of(x.shape) // RANK == group, x, 0.0)
    x = x + pltpu.roll(x, 64, 1)
    return x + pltpu.roll(x, 32, 1)


def panel_kernel(plan, order_hbm, g_hbm, e_hbm, wx_hbm, wb_hbm, wc_hbm, wd_hbm, top_ref, low_ref, mh_ref, ml_ref, m_ref, order_ref, g_ref, e_ref, wx_ref, wb_ref, wc_ref, wd_ref, dt_ref, w_ref, sems):
    rows = plan.rows
    total = plan.total
    shift = plan.shift

    small = [
        pltpu.make_async_copy(src, dst, sems.at[i])
        for i, (src, dst) in enumerate(
            ((order_hbm, order_ref), (wx_hbm, wx_ref), (wb_hbm, wb_ref), (wc_hbm, wc_ref), (wd_hbm, wd_ref))
        )
    ]
    big = []
    for i, (begin, end) in enumerate(plan.pieces):
        part = (slice(0, 1), slice(begin * LANES, min(end * LANES, total)))
        big.append(
            [
                pltpu.make_async_copy(src.at[part], dst.at[part], sems.at[5 + 2 * i + j])
                for j, (src, dst) in enumerate(((g_hbm, g_ref), (e_hbm, e_ref)))
            ]
        )
    small[0].start()
    for i, pair in enumerate(big):
        for copy in pair:
            copy.start()
        if i == 0:
            for copy in small[1:]:
                copy.start()
    small[0].wait()
    row, lane = starts_of(order_ref, plan.sizes)

    def merged(at, width):
        return g_ref[0:1, pl.ds(at, width)].astype(f32) + e_ref[0:1, pl.ds(at, width)].astype(f32)

    def fetch(base, count, stride, moved):
        step = {} if stride == 1 else {"stride": stride}
        now = m_ref[pl.ds(base, count, **step), :]
        return pltpu.roll(now, LANES - shift, 1) if moved else now

    def joined(base, count, stride, moved):
        now = fetch(base, count, stride, moved)
        if not moved:
            return now
        return jnp.where(lane_of((count, LANES)) < LANES - shift, now, fetch(base + 1, count, stride, moved))

    def either(k, work):
        for moved in (False, True):
            pl.when((lane[k] != 0) == moved)(functools.partial(work, moved))

    def put(at, count, column, tile):
        hi, lo = split2(tile)
        mh_ref[pl.ds(at, count), column : column + LANES] = hi
        ml_ref[pl.ds(at, count), column : column + LANES] = lo

    high = 64

    def read_x(first, last, moved):
        keep = lane_of((high, LANES)) < LANES - shift

        def block(i, _):
            base = row[0] + i * (high * CHUNKS)
            at = pl.multiple_of(i * high, high)
            now = fetch(base, high, CHUNKS, moved)
            for c in range(CHUNKS):
                tile = now
                if moved or c + 1 < CHUNKS:
                    now = fetch(base + (c + 1), high, CHUNKS, moved)
                if moved:
                    tile = jnp.where(keep, tile, now)
                put(at, high, c * LANES, tile)
            return 0

        lax.fori_loop(first, last, block, 0)

    done = 0
    for (begin, end), pair in zip(plan.pieces, big):
        for copy in pair:
            copy.wait()
        whole = min(end, total // LANES)

        def merge(i, _):
            r = pl.multiple_of(begin + i * MERGE, 8)
            m_ref[pl.ds(r, MERGE), :] = merged(pl.multiple_of(r * LANES, 1024), MERGE * LANES).reshape(MERGE, LANES)
            return 0

        count = (whole - begin) // MERGE
        lax.fori_loop(0, count, merge, 0)
        r = begin + count * MERGE
        n = (whole - r) // 8 * 8
        if n:
            m_ref[r : r + n, :] = merged(r * LANES, n * LANES).reshape(n, LANES)
        for r in range(r + n, whole):
            m_ref[r : r + 1, :] = merged(LANES * r, LANES)
        if end > whole:
            m_ref[whole : whole + 1, 0 : total % LANES] = merged(LANES * whole, total % LANES)

        ready = rows // high
        if end < plan.flat_rows:
            ready = jnp.minimum(lax.div(jnp.maximum(end - 1 - row[0], 0), jnp.int32(high * CHUNKS)), rows // high)
        either(0, functools.partial(read_x, done, ready))
        done = ready
    for copy in small[1:]:
        copy.wait()
    for k, column in ((1, COL_B), (2, COL_C)):
        either(k, lambda moved, k=k, column=column: put(0, rows, column, joined(row[k], rows, 1, moved)))

    groups = plan.dt_groups
    lanes_dt = lane_of((groups, LANES))

    def read_dt(moved):
        thirds = [joined(row[3] + q, groups, 3, moved) for q in range(3)]
        for b in range(8):
            q, s = divmod(NH * b, LANES)
            piece = thirds[q] if s == 0 else pltpu.roll(thirds[q], LANES - s, 1)
            if s + NH > LANES:
                piece = jnp.where(lanes_dt < LANES - s, piece, pltpu.roll(thirds[q + 1], LANES - s, 1))
            dt_ref[b * groups : (b + 1) * groups, :] = jnp.where(lanes_dt < NH, piece, 0.0)

    either(3, read_dt)
    put(0, rows, COL_DT, dt_ref[...])

    low = rows - plan.half

    def read_conv(moved):
        shape = (plan.conv_pad, LANES)
        conv = joined(row[4], plan.conv_pad, 1, moved)
        conv = jnp.where(lax.broadcasted_iota(jnp.int32, shape, 0) < plan.conv_rows, conv, 0.0)
        low_ref[low : low + plan.conv_pad, :] = conv

    either(4, read_conv)
    shape = (plan.vec_pad, LANES)
    place = lax.broadcasted_iota(jnp.int32, shape, 0) * LANES + lane_of(shape)
    vec = jnp.where(place < plan.sizes[5], m_ref[pl.ds(row[5], plan.vec_pad), :], 0.0)
    low_ref[low + plan.conv_pad :, :] = vec

    w_ref[...] = jnp.zeros_like(w_ref)
    w_ref[:, 0:NH] = wd_ref[...]
    panel = None
    lanes = lane_of((rows, LANES))
    for k, (w, column, width) in enumerate(
        ((wx_ref, 0, DI), (wb_ref, COL_B, DS), (wc_ref, COL_C, DS), (w_ref, COL_DT, LANES))
    ):
        hi, mid, lo = split3(w[...])
        none = jnp.zeros_like(hi)
        part = dot_nt(mh_ref[:, column : column + width], jnp.concatenate([hi, mid, lo, none], 0))
        part = part + dot_nt(ml_ref[:, column : column + width], jnp.concatenate([hi, mid, none, none], 0))
        part = part + pltpu.roll(part, 64, 1)
        part = part + pltpu.roll(part, 32, 1)
        panel = part if k == 0 else jnp.where(lanes >= RANK * k, part, panel)
    top_ref[...] = panel[0 : plan.half]
    low_ref[0:low, :] = panel[plan.half :]


def factor_kernel(plan, top_ref, low_ref, mh_ref, ml_ref, mine0_ref, mine1_ref, other_ref, z_ref):
    rows = plan.rows
    panel = jnp.concatenate([top_ref[...], low_ref[0 : rows - plan.half, :]], 0)
    group = lane_of((rows, LANES)) // RANK
    for k, column, width in ((0, 0, DI), (1, COL_B, DS), (2, COL_C, DS), (3, COL_DT, DS)):
        hi, mid, lo = (piece.astype(f32) for piece in split3(spread(panel, k)))
        two = jnp.where(group == 0, hi, jnp.where(group == 1, mid, 0.0))
        three = jnp.where(group == 2, lo, two).astype(bf16)
        two = two.astype(bf16)
        z = dot_tn(three, mh_ref[:, column : column + width]) + dot_tn(two, ml_ref[:, column : column + width])
        z_ref[:, column : column + width] = z[0:32] + z[32:64] + z[64:96]
    gram = lax.dot_general(
        panel, panel, (((0,), (0,)), ((), ())), preferred_element_type=f32, precision=lax.Precision.HIGHEST
    )
    group = lane_of((RANK, LANES)) // RANK
    out = gram[0:RANK]
    for k in range(1, 4):
        out = jnp.where(group == k, gram[RANK * k : RANK * (k + 1)], out)
    half = RANK // 2
    core = jnp.bitwise_and(lax.axis_index("mp"), 1)
    for mine in (0, 1):

        @pl.when(core == mine)
        def _():
            mine0_ref[:, 0:COLS] = z_ref[half * mine : half * mine + half // 2, :]
            mine1_ref[...] = z_ref[half * mine + half // 2 : half * (mine + 1), :]
            other_ref[:, 0:COLS] = z_ref[half * (1 - mine) : half * (2 - mine), :]

    other_ref[:, COLS:] = jnp.zeros((half, 4 * LANES), f32)
    for b in range(4):
        lanes = slice(COLS + b * LANES, COLS + (b + 1) * LANES)
        mine0_ref[:, lanes] = out[8 * b : 8 * (b + 1)]
        other_ref[0:8, lanes] = out[8 * b : 8 * (b + 1)]


def block_masks():
    square = (LANES, LANES)
    down = lax.broadcasted_iota(jnp.int32, square, 0)
    along = lane_of(square)
    return jnp.where(down == along, 1.0, 0.0), jnp.where(down // RANK == along // RANK, 1.0, 0.0)


def newton_schulz(eye, gram, turned, steps, last):
    for step in range(steps):
        mixing = ns_first * eye + ns_second * gram + ns_third * dot_exact(gram, gram)
        turned = mixing if turned is None else dot_exact(turned, mixing)
        if not (last and step + 1 == steps):
            gram = dot_exact(mixing, dot_exact(gram, mixing))
    return gram, turned


def begin_kernel(sum_ref, gram_out, turned_out, scale_out):
    eye, ones = block_masks()
    gram = [sum_ref[:, b * LANES : (b + 1) * LANES] for b in range(4)]
    gram = jnp.concatenate(gram * 4, 0) * ones
    trace = jnp.sum(gram * eye, axis=0, keepdims=True)
    trace = dot_exact(jnp.broadcast_to(trace, (8, LANES)), ones)
    scale = 1.0 / (jnp.sqrt(trace) + 1e-06)
    scale = scale * scale
    scale_out[...] = scale
    gram_out[...], turned_out[...] = newton_schulz(eye, gram * scale[0:1], None, NS_STEPS // 2, False)


def frame_kernel(plan, replicas, gram_ref, turned_ref, scale_ref, top_ref, low_ref, lhs_ref):
    rows = plan.rows
    eye, _ = block_masks()
    _, turned = newton_schulz(eye, gram_ref[...], turned_ref[...], NS_STEPS - NS_STEPS // 2, True)
    both = lax.dot_general(
        turned, turned, (((1,), (1,)), ((), ())), preferred_element_type=f32, precision=lax.Precision.HIGHEST
    )
    panel = jnp.concatenate([top_ref[...], low_ref[0 : rows - plan.half, :]], 0)
    left = dot_exact(panel, both * (scale_ref[0:1] * (1.0 / replicas)))
    group = lane_of((rows, LANES)) // RANK
    for k in range(4):
        hi, mid = (piece.astype(f32) for piece in split2(spread(left, k)))
        lhs_ref[k * rows : (k + 1) * rows, :] = jnp.where(group % 2 == 0, hi, mid).astype(bf16)


def output_kernel(plan, replicas, order_ref, mine0_ref, mine1_ref, other0_ref, other1_ref, lhs_ref, low_ref, m_ref, mom_ref, err_hbm, next_hbm, z_ref, t_ref, a_ref, x_ref, s_ref, err_ref, next_ref, sems):
    rows = plan.rows
    shift = plan.shift
    row, lane = starts_of(order_ref, plan.sizes)

    quarter = RANK // 4
    core = jnp.bitwise_and(lax.axis_index("mp"), 1)
    for mine in (0, 1):

        @pl.when(core == mine)
        def _():
            for i, ref in enumerate((mine0_ref, mine1_ref, other0_ref, other1_ref)):
                at = (2 * mine + i) % 4 * quarter
                z_ref[at : at + quarter, :] = ref[...]

    @pl.when(lane[0] != 0)
    def _():
        keep = lane_of((RANK, LANES)) >= shift
        before = jnp.zeros((RANK, LANES), f32)
        for c in range(CHUNKS):
            columns = slice(c * LANES, (c + 1) * LANES)
            now = pltpu.roll(z_ref[:, columns], shift, 1)
            z_ref[:, columns] = jnp.where(keep, now, before)
            before = now
        t_ref[...] = before

    def product(k, factor):
        hi, mid = split2(factor)
        return jnp.dot(
            lhs_ref[k * rows : (k + 1) * rows, :],
            jnp.concatenate([hi, hi, mid, mid], 0),
            preferred_element_type=f32,
        )

    for k, column, width in ((0, 0, DI), (1, COL_B, DS), (2, COL_C, DS), (3, COL_DT, DS)):
        x_ref[8 : 8 + rows, column : column + width] = product(k, z_ref[:, column : column + width])

    high = 32
    lanes1 = lane_of((1, LANES))

    def right(x):
        return pltpu.roll(x, shift, 1)

    def either(k, work):
        for moved in (False, True):
            pl.when((lane[k] != 0) == moved)(functools.partial(work, moved))

    def write_x(first, last, moved):
        keep = lane_of((high, LANES)) >= shift

        def block(i, _):
            at = pl.multiple_of(8 + i * high, 8)
            base = row[0] + i * (high * CHUNKS)
            for c in range(CHUNKS):
                now = x_ref[pl.ds(at, high), c * LANES : (c + 1) * LANES]
                if moved and c == 0:
                    now = jnp.where(keep, now, s_ref[pl.ds(at - 1, high), :])
                a_ref[pl.ds(base + c, high, stride=CHUNKS), :] = now
            return 0

        lax.fori_loop(first, last, block, 0)


    def place(k, ref, column, count):
        columns = slice(column, column + LANES)

        def work(moved):
            if not moved:
                a_ref[pl.ds(row[k], count), :] = ref[8 : 8 + count, columns]
                return
            head = right(ref[8:16, columns])[0:1]
            end = right(ref[count : count + 8, columns])[7:8]
            a_ref[pl.ds(row[k], 1), :] = jnp.where(lanes1 >= shift, head, a_ref[pl.ds(row[k], 1), :])
            final = row[k] + count
            a_ref[pl.ds(final, 1), :] = jnp.where(lanes1 < shift, end, a_ref[pl.ds(final, 1), :])
            n = count - 1
            now = right(ref[9 : 9 + n, columns])
            before = right(ref[8 : 8 + n, columns])
            a_ref[pl.ds(row[k] + 1, n), :] = jnp.where(lane_of((n, LANES)) >= shift, now, before)

        either(k, work)

    place(1, x_ref, COL_B, rows)
    place(2, x_ref, COL_C, rows)
    groups = plan.dt_groups
    lanes_dt = lane_of((groups, LANES))
    for q in range(3):
        third = jnp.zeros((groups, LANES), f32)
        for b in range(8):
            lo = NH * b - LANES * q
            if lo <= -NH or lo >= LANES:
                continue
            piece = x_ref[8 + b * groups : 8 + (b + 1) * groups, COL_DT : COL_DT + LANES]
            if lo % LANES:
                piece = pltpu.roll(piece, lo % LANES, 1)
            third = jnp.where((lanes_dt >= lo) & (lanes_dt < lo + NH), piece, third)
        s_ref[pl.ds(8 + q, groups, stride=3), :] = third
    place(3, s_ref, 0, 3 * groups)
    low = rows - plan.half
    s_ref[8 : 8 + plan.conv_pad, :] = low_ref[low : low + plan.conv_pad, :] * (1.0 / replicas)
    place(4, s_ref, 0, plan.conv_rows)
    vec = low_ref[low + plan.conv_pad :, :] * (1.0 / replicas)
    last = plan.vec_rows - 1
    a_ref[pl.ds(row[5], last), :] = vec[0:last]
    final = row[5] + last
    valid = plan.sizes[5] - last * LANES
    a_ref[pl.ds(final, 1), :] = jnp.where(lanes1 < valid, vec[last : last + 1], a_ref[pl.ds(final, 1), :])

    @pl.when(lane[0] != 0)
    def _():
        s_ref[8 : 8 + rows, :] = product(0, t_ref[...])
        s_ref[7:8, :] = a_ref[pl.ds(row[0], 1), :]
        final = row[0] + rows * CHUNKS
        end = s_ref[rows + 7 : rows + 8, :]
        a_ref[pl.ds(final, 1), :] = jnp.where(lanes1 < shift, end, a_ref[pl.ds(final, 1), :])

    total = plan.total
    spans = [(row[k] * LANES + lane[k], row[k] * LANES + lane[k] + plan.sizes[k]) for k in (4, 5)]

    def finish(at_row, count, width=LANES):
        n = count * width
        at = at_row * LANES
        a = a_ref[pl.ds(at_row, count), 0:width]
        next_ref[pl.ds(at, n)] = momentum_decay * mom_ref[pl.ds(at, n)] + a.reshape(n)
        near = [(at < end) & (at + n > begin) for begin, end in spans]
        near = near[0] | near[1]

        @pl.when(jnp.logical_not(near))
        def _():
            err = m_ref[pl.ds(at_row, count), 0:width] - a_ref[pl.ds(at_row, count), 0:width]
            err_ref[0:1, pl.ds(at, n)] = err.astype(bf16).reshape(1, n)

        @pl.when(near)
        def _():
            err = m_ref[pl.ds(at_row, count), 0:width] - a_ref[pl.ds(at_row, count), 0:width]
            index = lax.broadcasted_iota(jnp.int32, err.shape, 0) * LANES + lane_of(err.shape) + at
            for begin, end in spans:
                err = jnp.where((index >= begin) & (index < end), 0.0, err)
            err_ref[0:1, pl.ds(at, n)] = err.astype(bf16).reshape(1, n)

    copies = []
    done = 0
    for i, (begin, end) in enumerate(plan.pieces):
        step = high * CHUNKS
        ready = rows // high
        if end < plan.flat_rows:
            ready = jnp.minimum(lax.div(jnp.maximum(end - row[0], 0) + (step - 1), jnp.int32(step)), rows // high)
        either(0, functools.partial(write_x, done, ready))
        done = ready
        whole = min(end, total // LANES)
        count = (whole - begin) // FINISH
        lax.fori_loop(0, count, lambda j, _: (finish(pl.multiple_of(begin + j * FINISH, 8), FINISH), 0)[1], 0)
        r = begin + count * FINISH
        n = (whole - r) // 8 * 8
        if n:
            finish(r, n)
        for r in range(r + n, whole):
            finish(r, 1)
        if end > whole:
            finish(whole, 1, total % LANES)
        part = slice(begin * LANES, min(end * LANES, total))
        copies.append(pltpu.make_async_copy(err_ref.at[0:1, part], err_hbm.at[0:1, part], sems.at[2 * i]))
        copies.append(pltpu.make_async_copy(next_ref.at[part], next_hbm.at[part], sems.at[2 * i + 1]))
        for copy in copies[-2:]:
            copy.start()
    for copy in copies:
        copy.wait()


def specs(*spaces):
    return [pl.BlockSpec(memory_space=space) for space in spaces]


def pairwise(x, first, second):
    n = lax.axis_size("dp") * lax.axis_size("mp")
    return lax.ppermute(x, ("dp", "mp"), [(i, i ^ (second if i % 2 else first)) for i in range(n)])


def turned(steps, by):
    return steps[by:] + steps[:by]


def butterfly(halves, orders, first, last):
    for i in range(first, last):
        got = [pairwise(halves[h], orders[2 * h][i], orders[2 * h + 1][i]) for h in (0, 1)]
        halves = [mine + other for mine, other in zip(halves, got)]
    return halves


def body(grad_flat, error_flat, momentum_flat, warm_x, warm_b, warm_c, warm_dt, part_order):
    blocks = lax.axis_size("mp")
    replicas = lax.axis_size("dp")
    plan = Plan(blocks)
    rows = plan.rows
    total = plan.total
    shape = jax.ShapeDtypeStruct
    pieces = len(plan.pieces)
    dma = pltpu.SemaphoreType.DMA
    top, low, mh, ml, m = pl.pallas_call(
        functools.partial(panel_kernel, plan),
        out_shape=(
            shape((plan.half, LANES), f32),
            shape((plan.panel_rows - plan.half, LANES), f32),
            shape((rows, COLS), bf16),
            shape((rows, COLS), bf16),
            shape((plan.buf_rows, LANES), f32),
        ),
        in_specs=specs(*[HBM] * 7),
        out_specs=tuple(specs(*[VMEM] * 5)),
        scratch_shapes=[
            pltpu.SMEM((6,), jnp.int32),
            pltpu.VMEM((1, total), bf16),
            pltpu.VMEM((1, total), bf16),
            pltpu.VMEM((RANK, DI), f32),
            pltpu.VMEM((RANK, DS), f32),
            pltpu.VMEM((RANK, DS), f32),
            pltpu.VMEM((RANK, NH), f32),
            pltpu.VMEM((rows, LANES), f32),
            pltpu.VMEM((RANK, LANES), f32),
            dma((5 + 2 * pieces,)),
        ],
        compiler_params=pltpu.CompilerParams(vmem_limit_bytes=36 << 20),
        cost_estimate=pl.CostEstimate(flops=4 * rows * COLS * LANES, bytes_accessed=8 * total, transcendentals=0),
    )(*(pltpu.with_memory_space_constraint(x, HBM) for x in (part_order, grad_flat, error_flat, warm_x.T, warm_b.T, warm_c.T, warm_dt.T)))

    inner = [1 << b for b in range(1, (blocks - 1).bit_length())]
    outer = [blocks << b for b in range((replicas - 1).bit_length())]
    orders = [outer, turned(outer, len(outer) - 1), turned(outer, 1), outer]
    top, low = butterfly([top, low], orders, 0, len(outer))
    outer = outer[1:2] + outer[:1] + outer[2:]

    quarter, half = RANK // 4, RANK // 2
    mine0, mine1, other = pl.pallas_call(
        functools.partial(factor_kernel, plan),
        out_shape=(shape((quarter, WITH_GRAM), f32), shape((quarter, COLS), f32), shape((half, WITH_GRAM), f32)),
        in_specs=specs(*[VMEM] * 4),
        out_specs=tuple(specs(*[VMEM] * 3)),
        scratch_shapes=[pltpu.VMEM((RANK, COLS), f32)],
        compiler_params=pltpu.CompilerParams(vmem_limit_bytes=24 << 20),
        cost_estimate=pl.CostEstimate(flops=4 * rows * COLS * LANES, bytes_accessed=4 * total, transcendentals=0),
    )(top, low, mh, ml)
    got = pairwise(other, 1, 1)
    halves = [mine0 + got[:quarter], mine1 + got[quarter:, :COLS]]
    square = shape((LANES, LANES), f32)

    def begin(gram):
        return pl.pallas_call(
            begin_kernel,
            out_shape=(square, square, shape((8, LANES), f32)),
            in_specs=specs(VMEM),
            out_specs=tuple(specs(*[VMEM] * 3)),
            compiler_params=pltpu.CompilerParams(vmem_limit_bytes=4 << 20),
            cost_estimate=pl.CostEstimate(flops=1500000000, bytes_accessed=200000, transcendentals=0),
        )(gram)

    def frame(made):
        return pl.pallas_call(
            functools.partial(frame_kernel, plan, replicas),
            out_shape=shape((4 * rows, LANES), bf16),
            in_specs=specs(*[VMEM] * 5),
            out_specs=specs(VMEM)[0],
            compiler_params=pltpu.CompilerParams(vmem_limit_bytes=8 << 20),
            cost_estimate=pl.CostEstimate(flops=1500000000, bytes_accessed=600000, transcendentals=0),
        )(*made, top, low)

    gram, halves[0] = halves[0][:, COLS:], halves[0][:, :COLS]
    ring = inner + outer
    n = len(ring)
    orders = [turned(ring, by) for by in (0, n // 2, 1, 1 + n // 2)]
    halves = butterfly(halves, orders, 0, 1)
    halves[0], gram = lax.optimization_barrier((halves[0], gram))
    for bit in inner:
        gram = gram + pairwise(gram, bit, bit)
    halves = butterfly(halves, orders, 1, 2)
    halves[1], gram = lax.optimization_barrier((halves[1], gram))
    halves = butterfly(halves, orders, 2, 3)
    made = begin(gram)
    halves[0], made = lax.optimization_barrier((halves[0], made))
    lhs = frame(made)
    halves = butterfly(halves, orders, 3, n)
    halves[0], lhs = lax.optimization_barrier((halves[0], lhs))
    halves[1], lhs = lax.optimization_barrier((halves[1], lhs))
    others = [pairwise(half, 1, 1) for half in halves]

    return pl.pallas_call(
        functools.partial(output_kernel, plan, replicas),
        out_shape=(shape((1, total), bf16), shape((total,), f32)),
        in_specs=specs(pltpu.SMEM, *[VMEM] * 8),
        out_specs=tuple(specs(HBM, HBM)),
        scratch_shapes=[
            pltpu.VMEM((RANK, COLS), f32),
            pltpu.VMEM((RANK, LANES), f32),
            pltpu.VMEM((plan.buf_rows, LANES), f32),
            pltpu.VMEM((rows + 8, COLS), f32),
            pltpu.VMEM((rows + 24, LANES), f32),
            pltpu.VMEM((1, total), bf16),
            pltpu.VMEM((total,), f32),
            dma((2 * pieces,)),
        ],
        compiler_params=pltpu.CompilerParams(vmem_limit_bytes=36 << 20),
        cost_estimate=pl.CostEstimate(flops=2 * rows * COLS * LANES, bytes_accessed=16 * total, transcendentals=0),
    )(part_order, *halves, *others, lhs, low, m, momentum_flat)


def solution(mesh):
    placed = (P("dp", "mp"), P("dp", "mp"), P("mp"), P(), P(), P(), P(), P())
    return jax.shard_map(
        body, mesh=mesh, in_specs=placed, out_specs=(P("dp", "mp"), P("mp")), check_vma=False
    )
```
